128 devices in a mesh: fx: 16 (over x, z), fy: 8 (over y, core).
Axes of the slice: x: 4, y: 4, z: 4, core: 2. Of those that a mesh axis runs over, the one named last changes fastest.
Arguments:
- fluid_state: float32 [5, 8, 2048, 1024], P(None, None, 'fx', 'fy'), may hold values from -0.3 to 2.8, as said below
- surface_points: float32 [16384, 3, 128], P(('fx', 'fy')), may hold values from 0 to 1
- surface_normals: float32 [16384, 3, 128], P(('fx', 'fy')), may hold values from -1 to 1
- owner_ids: int32 [16384, 1], P(('fx', 'fy')), may hold values from 0 to 127; in each aligned block of 128 rows (0 to 127, 128 to 255, ...) at most 2 rows name the same one
- support_ids: int32 [16384, 2], P(('fx', 'fy')), may hold values from 0 to 7
- struct_points: float32 [1024, 3, 128], P(('fx', 'fy')), may hold values from 0 to 1
- couplings: float32 [1024, 4, 128, 128], P(('fx', 'fy')), may hold values from 0.5 to 1
- coupling_pattern: int32 [1024, 4], P(('fx', 'fy')), may hold values from 0 to 7, as said below
- stiff_diagonal: float32 [1024, 128], P(('fx', 'fy')), may hold values from 1.05 to 1.6
- struct_load: float32 [1024, 3, 128], P(('fx', 'fy')), may hold values from -6 to 6
- predicted: float32 [1024, 3, 128], P(('fx', 'fy')), may hold values from -3 to 3
- hist_residual: float32 [8, 1024, 3, 128], P(None, ('fx', 'fy')), may hold values from -0.03 to 0.03
- hist_response: float32 [8, 1024, 3, 128], P(None, ('fx', 'fy')), may hold values from -6 to 6
Outputs:
- new_state: float32 [5, 8, 2048, 1024], P(None, None, 'fx', 'fy')
- next_estimate: float32 [1024, 3, 128], P(('fx', 'fy'))
- coupling_residual: float32 [1024, 3, 128], P(('fx', 'fy'))
The draws below stay inside these ranges and needn't reach their ends.
Inputs may be any that keep to these rules, and one draw needn't show every extreme that they name: `fluid_state`: component 0 (density) lies in [0.8, 1.2], components 1 to 3 (momenta) in [-0.3, 0.3], component 4 (total energy) in [2.2, 2.8]. `owner_ids`: among the 128 surface blocks of one device (aligned blocks of rows), no owner is named by more than 2 of them. `support_ids`: local block numbers on the owner. For each device's 8 structure blocks and each column k, the entries coupling_pattern[., k] are a permutation of 0 to 7.
All inputs are finite; a program needn't handle non-finite values.
Results may differ from the reference program's by a relative error of at most 0.0003.
Values sent between devices are 32-bit elements; how exact they have to be, the bound alone decides.
No kernel may reach another device: no remote copies, remote signals or barrier semaphores. Data moves between devices by JAX's collectives and lax.ppermute only.
A program may use at most 192 MiB of HBM per device.

```python
import math
import jax
import jax.numpy as jnp
import numpy as np
from jax import lax

PTS = 128
CX = 128
CZ = 8
NBD = 8
KB = 4
KS = 2
HIST = 8
CG_ITERS = 2
COUPLE = 2
CY = 128
NX = 2048
NY = 1024
FB = 16384
CAP = 2
S_BLOCKS = 1024
N_FX = 16
N_FY = 8


def draw_fluid_state(key, part):
    first, second, third = jax.random.split(key, 3)
    shape = (CZ, NX, NY)
    density = jax.random.uniform(first, shape, jnp.float32, 0.8, 1.2)
    momentum = jax.random.uniform(second, (3,) + shape, jnp.float32, -0.3, 0.3)
    energy = jax.random.uniform(third, shape, jnp.float32, 2.2, 2.8)
    return jnp.concatenate([density[None], momentum, energy[None]], axis=0)


def draw_coupling_pattern(key, part):
    devices = S_BLOCKS // NBD
    subkeys = jax.random.split(key, devices * KB)
    orders = jax.vmap(lambda single: jax.random.permutation(single, NBD))(subkeys)
    orders = orders.reshape(devices, KB, NBD).transpose(0, 2, 1)
    return orders.reshape(S_BLOCKS, KB).astype(jnp.int32)


def set_ends(result, stream_key, least, largest):
    dims = result.shape
    place = [jax.random.randint(jax.random.fold_in(stream_key, axis), (), 0, dims[axis]) for axis in range(len(dims))]
    result = result.at[tuple(place)].set(least)
    longest = dims.index(max(dims))
    place[longest] = (place[longest] + 1) % dims[longest]
    return result.at[tuple(place)].set(largest)


def level_of(stream_key, shape, pieces, smallest, largest):
    factor_of = 1.0
    for dim, shards_of in pieces:
        steps = jax.random.uniform(jax.random.fold_in(jax.random.fold_in(stream_key, 6), dim), (shards_of,), jnp.float32, smallest / len(pieces), largest / len(pieces))
        factor_of = factor_of * jnp.repeat(jnp.exp(steps), shape[dim] // shards_of).reshape((-1,) + (1,) * (len(shape) - 1 - dim))
    return factor_of


def assign_block(key, own, number, rows, number_of, top, bound, skew):
    sequence = jax.random.permutation(key, number_of)
    packed, ordinary = portions_of(number_of, rows * top, bound, skew, True), portions_of(number_of, rows * top, bound, skew, False)
    places = jnp.arange(number_of)

    def named(lengths, rotation):
        used = int((lengths > 0).sum())
        fixed = max(1, used // 4)
        moved = fixed + (places - fixed + rotation * (used - fixed)) % max(1, number_of - fixed)
        return jnp.zeros((number_of,), jnp.int32).at[sequence[jnp.where(places < fixed, places, moved)]].set(jnp.asarray(lengths, jnp.int32))

    lengths = jnp.where(number % 4 == 0, named(packed, number // 4), named(ordinary, number - number // 4 - 1))
    mixed = jax.random.permutation(jax.random.fold_in(own, 3), number_of)
    source_of, sink = mixed[0:number_of // 2 * 2:2], mixed[1:number_of // 2 * 2:2]
    slack = jnp.minimum(lengths[source_of] - 1, bound - lengths[sink]) // 2
    slack = jnp.where((source_of == sequence[0]) | (sink == sequence[0]) | (lengths[sink] == 0), 0, jnp.maximum(slack, 0))
    moved = jax.random.randint(jax.random.fold_in(own, 4), (number_of // 2,), 0, 1 << 20) % (slack + 1)
    lengths = lengths.at[source_of].add(-moved).at[sink].add(moved)
    labels = jnp.searchsorted(jnp.cumsum(lengths), jnp.arange(rows * top), side="right").astype(jnp.int32)
    listing = labels.reshape(top, rows).T
    listing = listing[jax.random.permutation(jax.random.fold_in(own, 1), rows)]
    rotation = jax.random.randint(jax.random.fold_in(own, 2), (rows, 1), 0, top)
    return jnp.take_along_axis(listing, (jnp.arange(top)[None, :] + rotation) % top, axis=1)


def portions_of(amount, total, limit, slope, full):
    weights = [(1 << 20) // math.isqrt(standing ** slope) + 1 for standing in range(1, amount + 1)]
    largest = limit if full else min(limit, max(-(-total // amount), total * weights[0] // sum(weights)))
    least = 1 if total - largest >= amount - 1 else 0
    holding, rest = [largest] + [least] * (amount - 1), total - largest - least * (amount - 1)
    while rest > 0:
        free = [i for i in range(1, amount) if holding[i] < largest] or [i for i in range(1, amount) if holding[i] < limit]
        whole, remaining = sum([weights[i] for i in free]), rest
        for i in free:
            extra = min(limit - holding[i], max(1, remaining * weights[i] // whole), rest)
            holding[i] = holding[i] + extra
            rest = rest - extra
    return np.array(holding)


def centred(key, shape, deviation, bound, shards=(), dtype=jnp.bfloat16):
    level = level_of(key, shape, shards, -0.22, 0.18) if shards else 1.0
    entries = jax.random.normal(key, shape, jnp.float32) * deviation * level
    return jnp.minimum(jnp.maximum(entries, -bound), bound).astype(dtype)


def setup_inputs(seed: int = 0) -> dict:
    key_list = jax.random.split(jax.random.key(seed), 14)
    fluid_state = draw_fluid_state(jax.random.fold_in(key_list[13], 71), 0)
    surface_points = jnp.clip(1.0 * jax.random.uniform(key_list[1], (FB, 3, PTS), jnp.float32) ** level_of(key_list[1], (FB, 3, PTS), ((0, 128),), -0.2, 0.2), 0.0, 1.0)
    surface_normals = jnp.clip(jax.random.uniform(key_list[2], (FB, 3, PTS), jnp.float32, -1.0, 1.0) * level_of(key_list[2], (FB, 3, PTS), ((0, 128),), -0.4, 0.0), -1.0, 1.0)
    owner_ids_keys = jax.random.split(jax.random.fold_in(key_list[3], 1), FB // CX)
    owner_ids_turns = jax.random.permutation(jax.random.fold_in(key_list[3], 3), FB // CX)
    owner_ids = jax.vmap(lambda own, number: assign_block(jax.random.fold_in(key_list[3], 2), own, number, CX, N_FX * N_FY, 1, CAP, 2))(owner_ids_keys, owner_ids_turns).reshape((FB, 1))
    support_ids = set_ends(jax.random.randint(key_list[4], (FB, KS), 0, NBD), jax.random.fold_in(key_list[4], 1), 0, NBD - 1).astype(jnp.int32)
    struct_points = jnp.clip(1.0 * jax.random.uniform(key_list[5], (S_BLOCKS, 3, PTS), jnp.float32) ** level_of(key_list[5], (S_BLOCKS, 3, PTS), ((0, 128),), -0.2, 0.2), 0.0, 1.0)
    couplings = jnp.clip(0.5 + 0.5 * jax.random.uniform(key_list[6], (S_BLOCKS, KB, PTS, PTS), jnp.float32) ** level_of(key_list[6], (S_BLOCKS, KB, PTS, PTS), ((0, 128),), -0.2, 0.2), 0.5, 1.0)
    coupling_pattern = draw_coupling_pattern(jax.random.fold_in(key_list[13], 71), 0)
    stiff_diagonal = jnp.clip(1.05 + 0.5500001 * jax.random.uniform(key_list[8], (S_BLOCKS, PTS), jnp.float32) ** level_of(key_list[8], (S_BLOCKS, PTS), ((0, 128),), -0.2, 0.2), 1.05, 1.6)
    struct_load = centred(key_list[9], (S_BLOCKS, 3, PTS), 1.0, 6.0, ((0, 128),), jnp.float32)
    predicted = centred(key_list[10], (S_BLOCKS, 3, PTS), 0.5, 3.0, ((0, 128),), jnp.float32)
    hist_residual = centred(key_list[11], (HIST, S_BLOCKS, 3, PTS), 0.005, 0.03, ((1, 128),), jnp.float32)
    hist_response = centred(key_list[12], (HIST, S_BLOCKS, 3, PTS), 1.0, 6.0, ((1, 128),), jnp.float32)
    return {"fluid_state": fluid_state, "surface_points": surface_points, "surface_normals": surface_normals, "owner_ids": owner_ids, "support_ids": support_ids, "struct_points": struct_points, "couplings": couplings, "coupling_pattern": coupling_pattern, "stiff_diagonal": stiff_diagonal, "struct_load": struct_load, "predicted": predicted, "hist_residual": hist_residual, "hist_response": hist_response}


TOP_PRECISION = lax.Precision.HIGHEST
STEP_RATIO = 0.12
WALL_SPEED = 0.5
WALL_GAIN = 0.5
LOAD_SCALE = 4.0
PRESSURE_REF = 0.98
RADIUS = 1.0

def state_pressure(state):
    return 0.4 * (state[4] - 0.5 * (state[1] * state[1] + state[2] * state[2] + state[3] * state[3]) / state[0])

def face_terms(state, momentum):
    density = state[0]
    velocity = state[momentum] / density
    pressure = state_pressure(state)
    flux = state * velocity
    flux = flux.at[momentum].add(pressure)
    flux = flux.at[4].add(pressure * velocity)
    speed = jnp.abs(velocity) + jnp.sqrt(1.4 * pressure / density)
    return (flux, speed)

def rusanov(left, right, left_flux, right_flux, left_speed, right_speed):
    return 0.5 * (left_flux + right_flux) - 0.5 * jnp.maximum(left_speed, right_speed) * (right - left)

def vertical_terms(state, wall):
    bottom = state[:, 0]
    ghost = bottom.at[3].set(2.0 * bottom[0] * wall - bottom[3])
    column = jnp.concatenate([ghost[:, None], state, state[:, -1:]], axis=1)
    flux, speed = face_terms(column, 3)
    faces = rusanov(column[:, :-1], column[:, 1:], flux[:, :-1], flux[:, 1:], speed[:-1], speed[1:])
    return faces[:, 1:] - faces[:, :-1]

def fluid_section(state, wall):
    total = jnp.zeros_like(state)
    for axis, momentum in ((2, 1), (3, 2)):
        flux, speed = face_terms(state, momentum)
        faces = rusanov(state, jnp.roll(state, -1, axis), flux, jnp.roll(flux, -1, axis), speed, jnp.roll(speed, -1, axis - 1))
        total = total + (faces - jnp.roll(faces, 1, axis))
    total = total + vertical_terms(state, wall)
    return state - STEP_RATIO * total

def to_blocks(plane):
    return plane.reshape(N_FX, CX, N_FY, CY).transpose(0, 2, 1, 3).reshape(FB, CY)

def from_blocks(blocks):
    return blocks.reshape(N_FX, N_FY, CX, CY).transpose(0, 2, 1, 3).reshape(NX, NY)

def kernel_block(fluid_points, struct_nodes):
    squared = jnp.zeros((), jnp.float32)
    for axis in range(3):
        offset = fluid_points[..., axis, :, None] - struct_nodes[..., axis, None, :]
        squared = squared + offset * offset
    ratio = jnp.sqrt(squared) / RADIUS
    reach = jnp.maximum(1.0 - ratio, 0.0)
    return reach * reach * reach * reach * (4.0 * ratio + 1.0)

def mapped_motion(places, index, struct_points, field_values):
    group = math.gcd(FB, 128)

    def one_group(inputs):
        where, which = inputs
        kernel = kernel_block(where[:, None], struct_points[which])
        return jnp.einsum('gkij,gkcj->gci', kernel, field_values[which], precision=TOP_PRECISION)
    moved = lax.map(one_group, (places.reshape(-1, group, 3, PTS), index.reshape(-1, group, KS)))
    return moved.reshape(FB, 3, PTS)

def mapped_loads(places, index, struct_points, traction):
    group = math.gcd(FB, 128)

    def one_group(inputs):
        where, which, force = inputs
        kernel = kernel_block(where[:, None], struct_points[which])
        return jnp.einsum('gkij,gci->gkcj', kernel, force, precision=TOP_PRECISION)
    flux_terms = lax.map(one_group, (places.reshape(-1, group, 3, PTS), index.reshape(-1, group, KS), traction.reshape(-1, group, 3, PTS)))
    return jax.ops.segment_sum(flux_terms.reshape(FB * KS, 3, PTS), index.reshape(-1), num_segments=S_BLOCKS)

def stiffness(field_values, couplings, adjacent_cell, diagonal):
    scale = 1.0 / (2.0 * KB * PTS)
    forward_pass = jnp.einsum('hzwm,hzlm->hlw', couplings, field_values[adjacent_cell], precision=TOP_PRECISION)
    flux_terms = jnp.einsum('aosq,avs->aovq', couplings, field_values, precision=TOP_PRECISION)
    back = jax.ops.segment_sum(flux_terms.reshape(S_BLOCKS * KB, 3, PTS), adjacent_cell.reshape(-1), num_segments=S_BLOCKS)
    return diagonal[:, None, :] * field_values - scale * (forward_pass + back)

def conjugate(start, rhs, operate):
    residual = rhs - operate(start)
    direction = residual
    solution = start
    norm_now = jnp.sum(residual * residual)
    for count in range(CG_ITERS):
        image = operate(direction)
        alpha = norm_now / jnp.sum(direction * image)
        solution = solution + alpha * direction
        residual = residual - alpha * image
        if count + 1 < CG_ITERS:
            norm_next = jnp.sum(residual * residual)
            direction = residual + norm_next / norm_now * direction
            norm_now = norm_next
    return solution

def newton_update(response, gram, projected, responses):
    lower = jnp.linalg.cholesky(gram)
    middle = lax.linalg.triangular_solve(lower, projected[:, None], left_side=True, lower=True)
    weights = lax.linalg.triangular_solve(lower, middle, left_side=True, lower=True, transpose_a=True)[:, 0]
    return response - jnp.einsum('h,hbdp->bdp', weights, responses, precision=TOP_PRECISION)

def reference(fluid_state, surface_points, surface_normals, owner_ids, support_ids, struct_points, couplings, coupling_pattern, stiff_diagonal, struct_load, predicted, hist_residual, hist_response):
    devices = N_FX * N_FY
    index = (owner_ids * NBD + support_ids).astype(jnp.int32)
    prior_iterate = ((jnp.arange(S_BLOCKS) // NBD + devices - 1) % devices).astype(jnp.int32)
    adjacent_cell = (prior_iterate[:, None] * NBD + coupling_pattern).astype(jnp.int32)

    def operate(field_values):
        return stiffness(field_values, couplings, adjacent_cell, stiff_diagonal)
    estimate = predicted
    differences = hist_residual
    responses = hist_response
    last_residual = predicted
    last_response = predicted
    new_state = fluid_state
    residual = predicted
    for count in range(COUPLE):
        motion = mapped_motion(surface_points, index, struct_points, estimate)
        wall = from_blocks(WALL_SPEED * jnp.tanh(WALL_GAIN * lax.optimization_barrier(jnp.sum(surface_normals * motion, axis=1))))
        new_state = fluid_section(fluid_state, wall)
        pressure = to_blocks(state_pressure(new_state[:, 0]))
        traction = -LOAD_SCALE * (pressure - PRESSURE_REF)[:, None, :] * surface_normals
        loads = mapped_loads(surface_points, index, struct_points, traction)
        response = conjugate(estimate, struct_load + loads, operate)
        residual = response - estimate
        if count > 0:
            differences = jnp.concatenate([differences[1:], (residual - last_residual)[None]], axis=0)
            responses = jnp.concatenate([responses[1:], (response - last_response)[None]], axis=0)
        last_residual = residual
        last_response = response
        gram = jnp.einsum('hbdp,gbdp->hg', differences, differences, precision=TOP_PRECISION)
        projected = jnp.einsum('hbdp,bdp->h', differences, residual, precision=TOP_PRECISION)
        estimate = newton_update(response, gram, projected, responses)
    return (new_state, estimate, residual)
```

```python
import math

import jax
import jax.numpy as jnp
from jax import lax
from jax.sharding import PartitionSpec as P

COUPLE = 2


TOP_PRECISION = lax.Precision.HIGHEST
STEP_RATIO = 0.12
WALL_SPEED = 0.5
WALL_GAIN = 0.5
LOAD_SCALE = 4.0
PRESSURE_REF = 0.98
RADIUS = 1.0


def with_halo(cells, sides, width):
    for axis, dim in sides:
        count = lax.axis_size(axis)
        head = lax.slice_in_dim(cells, 0, width, axis=dim)
        tail = lax.slice_in_dim(cells, cells.shape[dim] - width, cells.shape[dim], axis=dim)
        cells = jnp.concatenate(
            [
                lax.ppermute(tail, axis, [(i, (i + 1) % count) for i in range(count)]),
                cells,
                lax.ppermute(head, axis, [((i + 1) % count, i) for i in range(count)]),
            ],
            axis=dim,
        )
    return cells


def state_pressure(state):
    return 0.4 * (
        state[4]
        - 0.5 * (state[1] * state[1] + state[2] * state[2] + state[3] * state[3]) / state[0]
    )


def face_terms(state, momentum):
    density = state[0]
    velocity = state[momentum] / density
    pressure = state_pressure(state)
    flux = state * velocity
    flux = flux.at[momentum].add(pressure)
    flux = flux.at[4].add(pressure * velocity)
    speed = jnp.abs(velocity) + jnp.sqrt(1.4 * pressure / density)
    return (flux, speed)


def rusanov(left, right, left_flux, right_flux, left_speed, right_speed):
    return 0.5 * (left_flux + right_flux) - 0.5 * jnp.maximum(left_speed, right_speed) * (
        right - left
    )


def vertical_terms(state, wall):
    bottom = state[:, 0]
    ghost = bottom.at[3].set(2.0 * bottom[0] * wall - bottom[3])
    column = jnp.concatenate([ghost[:, None], state, state[:, -1:]], axis=1)
    flux, speed = face_terms(column, 3)
    faces = rusanov(column[:, :-1], column[:, 1:], flux[:, :-1], flux[:, 1:], speed[:-1], speed[1:])
    return faces[:, 1:] - faces[:, :-1]


def horizontal_terms(state):
    extended = with_halo(state, (("fx", 2), ("fy", 3)), 1)
    strip = extended[:, :, :, 1:-1]
    flux, speed = face_terms(strip, 1)
    faces = rusanov(
        strip[:, :, :-1],
        strip[:, :, 1:],
        flux[:, :, :-1],
        flux[:, :, 1:],
        speed[:, :-1],
        speed[:, 1:],
    )
    total = faces[:, :, 1:] - faces[:, :, :-1]
    strip = extended[:, :, 1:-1, :]
    flux, speed = face_terms(strip, 2)
    faces = rusanov(
        strip[:, :, :, :-1],
        strip[:, :, :, 1:],
        flux[:, :, :, :-1],
        flux[:, :, :, 1:],
        speed[:, :, :-1],
        speed[:, :, 1:],
    )
    return total + (faces[:, :, :, 1:] - faces[:, :, :, :-1])


def kernel_block(fluid_points, struct_nodes):
    squared = jnp.zeros((), jnp.float32)
    for axis in range(3):
        offset = fluid_points[..., axis, :, None] - struct_nodes[..., axis, None, :]
        squared = squared + offset * offset
    ratio = jnp.sqrt(squared) / RADIUS
    reach = jnp.maximum(1.0 - ratio, 0.0)
    return reach * reach * reach * reach * (4.0 * ratio + 1.0)


def owner_kernels(places, support, struct_points):
    rows = places.shape[0]
    points = places.shape[-1]
    spread = support.shape[1]
    group = math.gcd(rows, 16)

    def one_group(inputs):
        where, which = inputs
        return kernel_block(where[:, None], struct_points[which])

    kernels = lax.map(
        one_group, (places.reshape(-1, group, 3, points), support.reshape(-1, group, spread))
    )
    return kernels.reshape(rows, spread, points, points)


def owner_motion(kernels, support, field_values):
    return jnp.einsum("gkij,gkcj->gci", kernels, field_values[support], precision=TOP_PRECISION)


def owner_loads(kernels, support, blocks, traction):
    flux_terms = jnp.einsum("gkij,gci->gkcj", kernels, traction, precision=TOP_PRECISION)
    selector = (support[:, :, None] == jnp.arange(blocks, dtype=jnp.int32)[None, None, :]).astype(
        jnp.float32
    )
    return jnp.einsum("rke,rkcj->ecj", selector, flux_terms, precision=TOP_PRECISION)


def route_coords(geometry, support):
    moved_geometry, moved_support = (
        lax.all_to_all(geometry, ("fx", "fy"), split_axis=0, concat_axis=0, tiled=True),
        lax.all_to_all(support, ("fx", "fy"), split_axis=0, concat_axis=0, tiled=True),
    )
    return (moved_geometry, moved_support)


def route_field(values):
    return lax.all_to_all(values, ("fx", "fy"), split_axis=0, concat_axis=0, tiled=True)


def stiffness(field_values, couplings, sparsity_layout, selector, diagonal):
    blocks = field_values.shape[0]
    scale = 1.0 / (2.0 * couplings.shape[1] * couplings.shape[2])
    flux_terms = jnp.einsum("aosq,avs->aovq", couplings, field_values, precision=TOP_PRECISION)
    shipped = jnp.einsum("bke,bkdj->edj", selector, flux_terms, precision=TOP_PRECISION)
    stacked = jnp.concatenate([shipped, field_values], axis=0)
    extended = with_halo(stacked, ((("fx", "fy"), 0),), blocks)
    prior_iterate = extended[:blocks]
    later = extended[-blocks:]
    forward_pass = jnp.einsum(
        "hzwm,hzlm->hlw", couplings, prior_iterate[sparsity_layout], precision=TOP_PRECISION
    )
    return diagonal[:, None, :] * field_values - scale * (forward_pass + later)


SHIFT = 1.25


def gathered_sums(row):
    spread = jnp.broadcast_to(row[None, :], (lax.axis_size(("fx", "fy")), row.shape[0]))
    return jnp.sum(
        lax.all_to_all(spread, ("fx", "fy"), split_axis=0, concat_axis=0, tiled=True), axis=0
    )


def dots(left, right):
    return jnp.einsum("hbdp,gbdp->hg", left, right, precision=TOP_PRECISION)


def combine(moments):
    m0, m1, m2, m3 = (moments[0], moments[1], moments[2], moments[3])
    alpha = m0 / (m1 + SHIFT * m0)
    gain = 1.0 - alpha * SHIFT
    norm = gain * gain * m0 - 2.0 * gain * alpha * m1 + alpha * alpha * m2
    mix = gain + norm / m0
    curve = (
        mix * mix * (m1 + SHIFT * m0)
        - 2.0 * mix * alpha * (m2 + SHIFT * m1)
        + alpha * alpha * (m3 + SHIFT * m2)
    )
    second = norm / curve
    return alpha + second * mix, -second * alpha


def newton_update(response, gram, projected, responses):
    lower = jnp.linalg.cholesky(gram)
    middle = lax.linalg.triangular_solve(lower, projected[:, None], left_side=True, lower=True)
    weights = lax.linalg.triangular_solve(
        lower, middle, left_side=True, lower=True, transpose_a=True
    )[:, 0]
    return response - jnp.einsum("h,hbdp->bdp", weights, responses, precision=TOP_PRECISION)


def on_device(
    fluid_state,
    surface_points,
    surface_normals,
    owner_ids,
    support_ids,
    struct_points,
    couplings,
    coupling_pattern,
    stiff_diagonal,
    struct_load,
    predicted,
    hist_residual,
    hist_response,
):
    rows_fx = lax.axis_size("fx")
    rows_fy = lax.axis_size("fy")
    devices = rows_fx * rows_fy
    surface_count = owner_ids.shape[0]
    capacity = max(2, 2 * surface_count // devices)
    owners = owner_ids[:, 0]
    chosen = (owners[:, None] == jnp.arange(devices, dtype=jnp.int32)[None, :]).astype(jnp.int32)
    slots = owners * capacity + jnp.sum((jnp.cumsum(chosen, axis=0) - chosen) * chosen, axis=1)
    width = devices * capacity

    def pack(values):
        return jnp.zeros((width,) + values.shape[1:], values.dtype).at[slots].set(values)

    owner_geometry, owner_support = route_coords(pack(surface_points), pack(support_ids))
    kernels = owner_kernels(owner_geometry, owner_support, struct_points)
    blocks = couplings.shape[0]
    selector = (
        coupling_pattern[:, :, None] == jnp.arange(blocks, dtype=jnp.int32)[None, None, :]
    ).astype(jnp.float32)

    def operate(field_values):
        return stiffness(field_values, couplings, coupling_pattern, selector, stiff_diagonal)

    horizontal = horizontal_terms(fluid_state)
    estimate = predicted
    responses = hist_response
    history = hist_residual.shape[0]
    new_state = fluid_state
    residual = predicted
    for count in range(COUPLE):
        motion_slots = owner_motion(kernels, owner_support, estimate)
        motion = route_field(motion_slots)[slots]
        wall = WALL_SPEED * jnp.tanh(WALL_GAIN * jnp.sum(surface_normals * motion, axis=1))
        new_state = fluid_state - STEP_RATIO * (horizontal + vertical_terms(fluid_state, wall))
        pressure = state_pressure(new_state[:, 0])
        traction = -LOAD_SCALE * (pressure - PRESSURE_REF)[:, None, :] * surface_normals
        owner_traction = route_field(pack(traction))
        loads = owner_loads(kernels, owner_support, blocks, owner_traction)
        start = struct_load + loads - operate(estimate)
        image = operate(start) - SHIFT * start
        basis = jnp.stack([start, image])
        third = jnp.sum(image * (operate(image) - SHIFT * image))
        if count == 0:
            tested = hist_residual
            own = dots(hist_residual, hist_residual).reshape(-1)
        else:
            tested = jnp.concatenate([hist_residual[1:], last_residual[None]], axis=0)
            own = jnp.zeros((history * history,), jnp.float32)
        pairs = dots(basis, jnp.concatenate([tested, basis]))
        row = jnp.concatenate([pairs.reshape(-1), third[None], own])
        row = jnp.pad(row, (0, 128 - row.shape[0]))
        totals = gathered_sums(row)
        span = history + 2
        pairs = totals[: 2 * span].reshape(2, span)
        m0, m1, m2 = pairs[0, history], pairs[0, history + 1], pairs[1, history + 1]
        first, second = combine((m0, m1, m2, totals[2 * span]))
        residual = first * start + second * image
        response = estimate + residual
        size = first * first * m0 + 2.0 * first * second * m1 + second * second * m2
        projected = first * pairs[0, :history] + second * pairs[1, :history]
        if count == 0:
            gram = totals[2 * span + 1 : 2 * span + 1 + history * history].reshape(
                history, history
            )
        else:
            overlap = projected[history - 1]
            newest = size - overlap
            edge = projected[: history - 1] - last_projected[1:]
            gram = jnp.concatenate(
                [
                    jnp.concatenate([last_gram[1:, 1:], edge[:, None]], axis=1),
                    jnp.concatenate([edge, (newest - overlap + last_size)[None]])[None],
                ],
                axis=0,
            )
            projected = jnp.concatenate([projected[: history - 1], newest[None]])
            responses = jnp.concatenate([responses[1:], (response - last_response)[None]], axis=0)
        last_gram, last_projected, last_size = gram, projected, size
        last_residual = residual
        last_response = response
        estimate = newton_update(response, gram, projected, responses)
    return (new_state, estimate, residual)


def solution(mesh):
    placed = (
        P(None, None, "fx", "fy"),
        P(("fx", "fy"), None, None),
        P(("fx", "fy"), None, None),
        P(("fx", "fy"), None),
        P(("fx", "fy"), None),
        P(("fx", "fy"), None, None),
        P(("fx", "fy"), None, None, None),
        P(("fx", "fy"), None),
        P(("fx", "fy"), None),
        P(("fx", "fy"), None, None),
        P(("fx", "fy"), None, None),
        P(None, ("fx", "fy"), None, None),
        P(None, ("fx", "fy"), None, None),
    )
    return jax.shard_map(
        on_device,
        mesh=mesh,
        in_specs=placed,
        out_specs=(
            P(None, None, "fx", "fy"),
            P(("fx", "fy"), None, None),
            P(("fx", "fy"), None, None),
        ),
        check_vma=False,
    )
```

```python
import functools

import jax
import jax.numpy as jnp
from jax import lax
from jax.experimental import pallas as pl
from jax.experimental.pallas import tpu as pltpu
from jax.sharding import PartitionSpec as P

AXES = ("fx", "fy")
DEVICES = 128
TOP_PRECISION = lax.Precision.HIGHEST
STEP_RATIO = 0.12
WALL_SPEED = 0.5
WALL_GAIN = 0.5
LOAD_SCALE = 4.0
PRESSURE_REF = 0.98
SHIFT = 1.25
PEERS = 4
F32 = jnp.float32
BF16 = jnp.bfloat16
VMEM = pltpu.VMEM
SMEM = pltpu.SMEM


def with_halo(cells, sides, width):
    for axis, dim in sides:
        count = lax.axis_size(axis)
        head = lax.slice_in_dim(cells, 0, width, axis=dim)
        tail = lax.slice_in_dim(cells, cells.shape[dim] - width, cells.shape[dim], axis=dim)
        cells = jnp.concatenate(
            [
                lax.ppermute(tail, axis, [(i, (i + 1) % count) for i in range(count)]),
                cells,
                lax.ppermute(head, axis, [((i + 1) % count, i) for i in range(count)]),
            ],
            axis=dim,
        )
    return cells


def state_pressure(state):
    return 0.4 * (
        state[4]
        - 0.5 * (state[1] * state[1] + state[2] * state[2] + state[3] * state[3]) / state[0]
    )


def face_terms(state, momentum):
    density = state[0]
    velocity = state[momentum] / density
    pressure = state_pressure(state)
    flux = state * velocity
    flux = flux.at[momentum].add(pressure)
    flux = flux.at[4].add(pressure * velocity)
    speed = jnp.abs(velocity) + jnp.sqrt(1.4 * pressure / density)
    return (flux, speed)


def rusanov(left, right, left_flux, right_flux, left_speed, right_speed):
    return 0.5 * (left_flux + right_flux) - 0.5 * jnp.maximum(left_speed, right_speed) * (
        right - left
    )


def vertical_terms(state):
    column = jnp.concatenate([state, state[:, -1:]], axis=1)
    flux, speed = face_terms(column, 3)
    faces = rusanov(column[:, :-1], column[:, 1:], flux[:, :-1], flux[:, 1:], speed[:-1], speed[1:])
    return faces - jnp.concatenate([jnp.zeros_like(faces[:, :1]), faces[:, :-1]], axis=1)


def horizontal_terms(state):
    extended = with_halo(state, (("fx", 2), ("fy", 3)), 1)
    strip = extended[:, :, :, 1:-1]
    flux, speed = face_terms(strip, 1)
    faces = rusanov(
        strip[:, :, :-1],
        strip[:, :, 1:],
        flux[:, :, :-1],
        flux[:, :, 1:],
        speed[:, :-1],
        speed[:, 1:],
    )
    total = faces[:, :, 1:] - faces[:, :, :-1]
    strip = extended[:, :, 1:-1, :]
    flux, speed = face_terms(strip, 2)
    faces = rusanov(
        strip[:, :, :, :-1],
        strip[:, :, :, 1:],
        flux[:, :, :, :-1],
        flux[:, :, :, 1:],
        speed[:, :, :-1],
        speed[:, :, 1:],
    )
    return total + (faces[:, :, :, 1:] - faces[:, :, :, :-1])


def iota(shape, dim):
    return lax.broadcasted_iota(jnp.int32, shape, dim)


def exact_dot(left, right):
    return jnp.dot(left, right, precision=TOP_PRECISION, preferred_element_type=F32)


def dot_nn(left, right):
    return lax.dot_general(left, right, (((1,), (0,)), ((), ())), preferred_element_type=F32)


def dot_nt(left, right):
    return lax.dot_general(left, right, (((1,), (1,)), ((), ())), preferred_element_type=F32)


def halves(value):
    high = value.astype(BF16)
    return high, (value - high.astype(F32)).astype(BF16)


def stacked_halves(value):
    high = value.astype(BF16).astype(F32)
    return jnp.concatenate([high, value - high], axis=0).astype(BF16)


def pack_kernel(own, points, normals, support, geo, packed_normals, slot_row, slot_col):
    across = jnp.broadcast_to(own[...].astype(F32), (128, 128))
    along = across.T
    same = across == along
    row_rank = jnp.sum(jnp.where(same & (iota((128, 128), 0) < iota((128, 128), 1)), 1.0, 0.0), axis=0, keepdims=True)
    col_rank = jnp.sum(jnp.where(same & (iota((128, 128), 1) < iota((128, 128), 0)), 1.0, 0.0), axis=1, keepdims=True)
    slots = 2.0 * along[:1] + row_rank
    slot_row[...] = jnp.broadcast_to(slots, (8, 128))
    slot_col[...] = 2.0 * across + col_rank
    index = iota((1024, 128), 0)
    peer, kind = index // 8, index % 8
    rank = jnp.where(kind < 6, kind // 3, kind - 6)
    part = jnp.where(kind < 6, kind % 3, 3)
    hit = slots == (2 * peer + rank).astype(F32)
    ids = jnp.concatenate([support[...].astype(F32), jnp.zeros((128, 126), F32)], axis=1)
    total = exact_dot(jnp.where(hit & (part == 3), 1.0, 0.0), ids)
    other = jnp.zeros((1024, 128), F32)
    for axis in range(3):
        chosen = jnp.where(hit & (part == axis), 1.0, 0.0)
        total = total + exact_dot(chosen, points[:, axis, :])
        other = other + exact_dot(chosen, normals[:, axis, :])
    geo[...] = total
    packed_normals[...] = other


def node_table(struct_points):
    def cut(value):
        return lax.reduce_precision(value, 8, 7)

    centred = struct_points - 0.5
    norm = jnp.sum(centred * centred, axis=1)
    nodes = -2.0 * jnp.transpose(centred, (0, 2, 1))
    zero = jnp.zeros_like(nodes[..., :1])
    tables = []
    for rank in range(2):
        cols = [zero] * 8
        for axis in range(3):
            cols[3 * rank + axis] = nodes[..., axis : axis + 1]
        cols[6 + rank] = zero + 1.0
        full = jnp.concatenate(cols, axis=-1)
        high = cut(full)
        mid = cut(full - high)
        low = cut(full - high - mid)
        size = norm[..., None]
        size_high = cut(size)
        size_mid = cut(size - size_high)
        size_low = cut(size - size_high - size_mid)
        rest = [size_high, size_mid, size_low] + [zero] * 13
        tables.append(jnp.concatenate([high, mid, low, high, mid, high] + rest, axis=-1))
    return jnp.stack(tables).reshape(16, 128, 64).astype(BF16)


def phi_kernel(support, geo, normals, table, field, phi_high, phi_low, motion, stack):
    step = pl.program_id(0)

    @pl.when(step == 0)
    def _():
        for block in range(8):
            stack[block] = stacked_halves(field[pl.ds(block * 8, 8), :])

    row = iota((8, 128), 0)
    rows = []
    for peer in range(PEERS):
        tile = geo[pl.ds(peer * 8, 8), :] - 0.5
        square = tile * tile
        first = jnp.sum(jnp.where(row < 3, square, 0.0), axis=0, keepdims=True)
        second = jnp.sum(jnp.where((row >= 3) & (row < 6), square, 0.0), axis=0, keepdims=True)
        places = jnp.where(row < 6, tile, jnp.where(row == 6, first, second))
        high = places.astype(BF16).astype(F32)
        mid = (places - high).astype(BF16).astype(F32)
        low = places - high - mid
        right = jnp.concatenate(
            [high, high, high, mid, mid, low, jnp.ones((8, 128), F32), jnp.zeros((8, 128), F32)],
            axis=0,
        ).astype(BF16)
        for rank in range(2):
            slot = peer * 2 + rank
            moved = jnp.zeros((16, 128), F32)
            for k in range(2):
                block = support[(step * PEERS * 2 + slot) * 2 + k]
                squared = jnp.maximum(dot_nn(table[rank * 8 + block], right), 1e-30)
                ratio = squared * lax.rsqrt(squared)
                reach = jnp.maximum(1.0 - ratio, 0.0)
                reach = reach * reach
                phi = reach * reach * (4.0 * ratio + 1.0)
                upper, lower = halves(phi)
                phi_high[slot * 2 + k] = upper
                phi_low[slot * 2 + k] = lower
                moved = moved + dot_nn(stack[block], upper) + dot_nn(stack[block], lower)
            both = moved[:8] + moved[8:]
            rows.append(
                jnp.sum(
                    both[:3] * normals[pl.ds(peer * 8 + 3 * rank, 3), :], axis=0, keepdims=True
                )
            )
    motion[...] = jnp.concatenate(rows, axis=0)


def motion_kernel(support, normals, field, phi_high, phi_low, motion, stack):
    step = pl.program_id(0)

    @pl.when(step == 0)
    def _():
        for block in range(8):
            stack[block] = stacked_halves(field[pl.ds(block * 8, 8), :])

    rows = []
    for slot in range(2 * PEERS):
        moved = jnp.zeros((16, 128), F32)
        for k in range(2):
            block = support[(step * PEERS * 2 + slot) * 2 + k]
            moved = (
                moved
                + dot_nn(stack[block], phi_high[slot * 2 + k])
                + dot_nn(stack[block], phi_low[slot * 2 + k])
            )
        both = moved[:8] + moved[8:]
        rows.append(
            jnp.sum(
                both[:3] * normals[pl.ds(slot // 2 * 8 + 3 * (slot % 2), 3), :],
                axis=0,
                keepdims=True,
            )
        )
    motion[...] = jnp.concatenate(rows, axis=0)


def wall_kernel(received, slot_row, slot_col, bottom, base, fresh, sent):
    lanes = iota((128, 256), 1).astype(F32)
    column = jnp.concatenate([slot_col[...], slot_col[...]], axis=1)
    argument = exact_dot(jnp.where(column == lanes, 1.0, 0.0), received[...])
    wall = WALL_SPEED * jnp.tanh(WALL_GAIN * argument)
    lower = [bottom[part] for part in range(5)]
    ghost = [lower[0], lower[1], lower[2], 2.0 * lower[0] * wall - lower[3], lower[4]]
    inverse = 1.0 / lower[0]

    def terms(state):
        velocity = state[3] * inverse
        pressure = 0.4 * (
            state[4]
            - 0.5 * (state[1] * state[1] + state[2] * state[2] + state[3] * state[3]) * inverse
        )
        flux = [part * velocity for part in state]
        flux[3] = flux[3] + pressure
        flux[4] = flux[4] + pressure * velocity
        return flux, jnp.abs(velocity) + jnp.sqrt(1.4 * pressure * inverse)

    ghost_flux, ghost_speed = terms(ghost)
    lower_flux, lower_speed = terms(lower)
    speed = jnp.maximum(ghost_speed, lower_speed)
    new = []
    for part in range(5):
        face = 0.5 * (ghost_flux[part] + lower_flux[part])
        if part == 3:
            face = face - 0.5 * speed * (lower[3] - ghost[3])
        new.append(base[part] + STEP_RATIO * face)
        fresh[part] = new[part]
    pressure = 0.4 * (
        new[4] - 0.5 * (new[1] * new[1] + new[2] * new[2] + new[3] * new[3]) / new[0]
    )
    amount = -LOAD_SCALE * (pressure - PRESSURE_REF)
    chosen = jnp.where(slot_row[:1] == iota((256, 128), 0).astype(F32), 1.0, 0.0)
    sent[...] = exact_dot(chosen, amount)


def spread_back(values, couplings, pattern, total):
    total[...] = jnp.zeros((64, 128), F32)

    def body(block, carry):
        stack = stacked_halves(values[pl.ds(pl.multiple_of(block * 8, 8), 8), :])
        for k in range(4):
            upper, lower = halves(couplings[block, k])
            term = dot_nn(stack, upper) + dot_nn(stack, lower)
            place = pl.ds(pl.multiple_of(pattern[block * 4 + k] * 8, 8), 8)
            total[place, :] = total[place, :] + term[:8] + term[8:]
        return carry

    lax.fori_loop(0, 8, body, 0)


def gather_forward(values, couplings, pattern, total):
    def body(block, carry):
        term = jnp.zeros((16, 128), F32)
        for k in range(4):
            place = pl.ds(pl.multiple_of(pattern[block * 4 + k] * 8, 8), 8)
            stack = stacked_halves(values[place, :])
            upper, lower = halves(couplings[block, k])
            term = term + dot_nt(stack, upper) + dot_nt(stack, lower)
        total[pl.ds(pl.multiple_of(block * 8, 8), 8), :] = term[:8] + term[8:]
        return carry

    lax.fori_loop(0, 8, body, 0)


def back_kernel(pattern, values, couplings, total):
    spread_back(values, couplings, pattern, total)


def loads_kernel(
    support, pattern, amounts, normals, phi_high, phi_low, base, couplings, start, back, loads
):
    step = pl.program_id(0)

    @pl.when(step == 0)
    def _():
        loads[...] = jnp.zeros((8, 8, 128), F32)

    row = iota((8, 128), 0)
    for peer in range(PEERS):
        tile = normals[pl.ds(peer * 8, 8), :]
        for rank in range(2):
            slot = peer * 2 + rank
            kept = (row >= 3 * rank) & (row < 3 * rank + 3)
            force = jnp.where(kept, tile * amounts[pl.ds(slot, 1), :], 0.0)
            stack = stacked_halves(force)
            for k in range(2):
                block = support[(step * PEERS * 2 + slot) * 2 + k]
                term = dot_nt(stack, phi_high[slot * 2 + k]) + dot_nt(stack, phi_low[slot * 2 + k])
                loads[block] = loads[block] + term[:8] + term[8:]

    @pl.when(step == pl.num_programs(0) - 1)
    def _():
        for block in range(8):
            tile = loads[block]
            start[pl.ds(block * 8, 8), :] = base[pl.ds(block * 8, 8), :] + jnp.where(
                row < 3, tile + pltpu.roll(tile, 5, 0), 0.0
            )
        spread_back(start, couplings, pattern, back)


def apply_kernel(shift, pattern, values, before, behind, diagonal, couplings, image, work):
    gather_forward(before, couplings, pattern, work)
    image[...] = (diagonal[...] - shift) * values[...] - (1.0 / 1024.0) * (
        work[...] + behind[...]
    )


def row_sum(value):
    return jnp.sum(value, axis=0, keepdims=True)


def sums_kernel(
    pattern, start, image, before, diagonal, couplings, tested, extra, own, row, work, stack
):
    gather_forward(before, couplings, pattern, work)
    first, second = start[...], image[...]
    stack[...] = jnp.zeros((128, 128), F32)
    for h in range(8):
        stack[pl.ds(h, 1), :] = row_sum(tested[h] * first)
        stack[pl.ds(8 + h, 1), :] = row_sum(tested[h] * second)
    third = second * ((diagonal[...] - SHIFT) * second - (2.0 / 1024.0) * work[...])
    stack[pl.ds(16, 1), :] = row_sum(first * first)
    stack[pl.ds(17, 1), :] = row_sum(first * second)
    stack[pl.ds(18, 1), :] = row_sum(second * second)
    stack[pl.ds(19, 1), :] = row_sum(third)
    stack[pl.ds(20, 1), :] = row_sum(extra[...] * first)
    stack[pl.ds(21, 1), :] = row_sum(extra[...] * second)
    sums = lax.dot_general(
        jnp.ones((8, 128), F32),
        stack[...],
        (((1,), (1,)), ((), ())),
        precision=TOP_PRECISION,
        preferred_element_type=F32,
    )
    row[...] = jnp.broadcast_to(sums[:1] + own[...], (128, 128))


def solve_kernel(
    count, received, memory, field, start, image, last, responses, estimate, residual, *more
):
    totals = row_sum(received[...])

    def lane(index):
        return totals[:, index : index + 1]

    lanes, row = iota((8, 128), 1), iota((8, 128), 0)

    def column(values):
        return jnp.sum(
            jnp.where(lanes == row, jnp.broadcast_to(values, (8, 128)), 0.0), axis=1, keepdims=True
        )

    m0, m1, m2, m3 = lane(16), lane(17), lane(18), lane(19)
    alpha = m0 / (m1 + SHIFT * m0)
    gain = 1.0 - alpha * SHIFT
    norm = gain * gain * m0 - 2.0 * gain * alpha * m1 + alpha * alpha * m2
    mix = gain + norm / m0
    curve = (
        mix * mix * (m1 + SHIFT * m0)
        - 2.0 * mix * alpha * (m2 + SHIFT * m1)
        + alpha * alpha * (m3 + SHIFT * m2)
    )
    follow = norm / curve
    c0 = alpha + follow * mix
    c1 = -follow * alpha
    change = c0 * start[...] + c1 * image[...]
    response = field[...] + change
    size = c0 * c0 * m0 + 2.0 * c0 * c1 * m1 + c1 * c1 * m2
    projected = c0 * totals + c1 * pltpu.roll(totals, 120, 1)
    lane_row = iota((1, 128), 1)
    if count == 0:
        picked = jnp.where(
            (lanes >= 64 + 8 * row) & (lanes < 72 + 8 * row),
            jnp.broadcast_to(totals, (8, 128)),
            0.0,
        )
        fold = jnp.where(
            (iota((128, 128), 0) >= 64) & (iota((128, 128), 0) % 8 == iota((128, 128), 1)), 1.0, 0.0
        )
        gram = exact_dot(picked, fold)
    else:
        overlap = c0 * lane(20) + c1 * lane(21)
        newest = size - overlap
        edge = projected - memory[8:9, :]
        edge = jnp.where(lane_row == 0, newest - overlap + memory[9:10, :1], edge)
        projected = jnp.where(lane_row == 0, newest, projected)
        gram = jnp.where(
            row == 0, jnp.broadcast_to(edge, (8, 128)), jnp.where(lanes == 0, column(edge), memory[:8, :])
        )
    system = jnp.where(lanes < 8, gram, jnp.where(lanes == 8, column(projected), 0.0))
    for j in range(8):
        pivot = system[j : j + 1] / system[j : j + 1, j : j + 1]
        system = jnp.where(row == j, pivot, system - system[:, j : j + 1] * pivot)
    result = response
    for h in range(8):
        weight = system[h : h + 1, 8:9]
        used = responses[h] if count == 0 or h > 0 else response - last[...]
        result = result - weight * used
    if count == 0:
        kept, saved = more
        estimate[...] = result
        residual[...] = change
        kept[...] = response
        saved[:8, :] = gram
        saved[8:16, :] = jnp.where(
            row == 0, jnp.broadcast_to(projected, (8, 128)), jnp.where(row == 1, size, 0.0)
        )
    else:
        for block in range(8):
            estimate[block] = result[block * 8 : block * 8 + 3]
            residual[block] = change[block * 8 : block * 8 + 3]


def shape(*dims, dtype=F32):
    return jax.ShapeDtypeStruct(dims, dtype)


def call(kernel, outs, scratch=(), scalars=0, cost=None, **kw):
    specs = [pl.BlockSpec(memory_space=SMEM)] * scalars

    def run(*args):
        return pl.pallas_call(
            kernel,
            out_shape=outs,
            in_specs=specs + [pl.BlockSpec(memory_space=VMEM)] * (len(args) - scalars),
            out_specs=jax.tree.map(lambda _: pl.BlockSpec(memory_space=VMEM), outs),
            scratch_shapes=list(scratch),
            compiler_params=pltpu.CompilerParams(vmem_limit_bytes=24 << 20),
            cost_estimate=cost,
            **kw,
        )(*args)

    return run


def exchange(values):
    return lax.all_to_all(values, AXES, split_axis=0, concat_axis=0, tiled=True)


def forward(values):
    return lax.ppermute(values, AXES, [(i, (i + 1) % DEVICES) for i in range(DEVICES)])


def backward(values):
    return lax.ppermute(values, AXES, [((i + 1) % DEVICES, i) for i in range(DEVICES)])


STEPS = DEVICES // PEERS
WHOLE = dict(memory_space=VMEM)
TILES = pl.BlockSpec((4 * PEERS, 128, 128), lambda i, *_: (i, 0, 0))


def fixed(*dims):
    return pl.BlockSpec(dims, lambda i, *_: (0,) * len(dims))


def per_step(rows):
    return pl.BlockSpec((rows, 128), lambda i, *_: (i, 0))


def streaming(kernel, scalars, in_specs, out_specs, outs, scratch, cost, args):
    return pl.pallas_call(
        kernel,
        out_shape=outs,
        grid_spec=pltpu.PrefetchScalarGridSpec(
            num_scalar_prefetch=scalars,
            grid=(STEPS,),
            in_specs=in_specs,
            out_specs=out_specs,
            scratch_shapes=scratch,
        ),
        compiler_params=pltpu.CompilerParams(
            dimension_semantics=("arbitrary",), vmem_limit_bytes=32 << 20
        ),
        cost_estimate=cost,
    )(*args)


PHI_BYTES = 512 * 128 * 128 * 4
PHI_COST = pl.CostEstimate(flops=2 * 512 * 128 * 128 * 48, bytes_accessed=PHI_BYTES, transcendentals=0)


def build_phi(support, geo, normals, table, field):
    return streaming(
        phi_kernel,
        1,
        [per_step(8 * PEERS), per_step(8 * PEERS), fixed(16, 128, 64), fixed(64, 128)],
        [TILES, TILES, per_step(2 * PEERS)],
        [
            shape(512, 128, 128, dtype=BF16),
            shape(512, 128, 128, dtype=BF16),
            shape(256, 128),
        ],
        [pltpu.VMEM((8, 16, 128), BF16)],
        PHI_COST,
        (support, geo, normals, table, field),
    )


def find_motion(support, normals, field, phi_high, phi_low):
    return streaming(
        motion_kernel,
        1,
        [per_step(8 * PEERS), fixed(64, 128), TILES, TILES],
        per_step(2 * PEERS),
        shape(256, 128),
        [pltpu.VMEM((8, 16, 128), BF16)],
        PHI_COST,
        (support, normals, field, phi_high, phi_low),
    )


def find_loads(support, pattern, amounts, normals, phi_high, phi_low, base, couplings):
    return streaming(
        loads_kernel,
        2,
        [
            per_step(2 * PEERS),
            per_step(8 * PEERS),
            TILES,
            TILES,
            fixed(64, 128),
            fixed(8, 4, 128, 128),
        ],
        [fixed(64, 128), fixed(64, 128)],
        [shape(64, 128), shape(64, 128)],
        [pltpu.VMEM((8, 8, 128), F32)],
        PHI_COST,
        (support, pattern, amounts, normals, phi_high, phi_low, base, couplings),
    )


def padded(values):
    wide = [(0, 0)] * (values.ndim - 2) + [(0, 5), (0, 0)]
    values = jnp.pad(values, wide)
    return values.reshape(values.shape[:-3] + (64, 128))


def on_device(
    fluid_state,
    surface_points,
    surface_normals,
    owner_ids,
    support_ids,
    struct_points,
    couplings,
    coupling_pattern,
    stiff_diagonal,
    struct_load,
    predicted,
    hist_residual,
    hist_response,
):
    pattern = coupling_pattern.reshape(32)
    geo, normals, slot_row, slot_col = call(
        pack_kernel, [shape(1024, 128), shape(1024, 128), shape(8, 128), shape(128, 128)]
    )(owner_ids, surface_points, surface_normals, support_ids)
    geo = exchange(geo)
    normals = exchange(normals)
    support = geo.reshape(128, 8, 128)[:, 6:, :2].astype(jnp.int32).reshape(512)
    diagonal = padded(jnp.broadcast_to(stiff_diagonal[:, None, :], (8, 3, 128)))
    load = padded(struct_load)
    field = padded(predicted)
    tested = padded(hist_residual)
    responses = padded(hist_response)
    own = jnp.pad(
        jnp.einsum("hbdp,gbdp->hg", hist_residual, hist_residual, precision=TOP_PRECISION).reshape(
            1, 64
        ),
        ((0, 0), (64, 0)),
    )
    table = node_table(struct_points)

    def back_of(values):
        return call(back_kernel, shape(64, 128), scalars=1)(pattern, values, couplings)

    def applied(values, back, shift):
        return call(
            functools.partial(apply_kernel, shift),
            shape(64, 128),
            [pltpu.VMEM((64, 128), F32)],
            scalars=1,
        )(pattern, values, forward(values), backward(back), diagonal, couplings)

    phi_high, phi_low, motion = build_phi(support, geo, normals, table, field)
    base_state = fluid_state - STEP_RATIO * (
        horizontal_terms(fluid_state) + vertical_terms(fluid_state)
    )
    bottom = fluid_state[:, 0]
    base_bottom = base_state[:, 0]
    extra = field
    memory = diagonal
    last = field
    for count in range(2):
        if count > 0:
            motion = find_motion(support, normals, field, phi_high, phi_low)
        received = exchange(motion)
        base = load - applied(field, back_of(field), 0.0)
        fresh, sent = call(wall_kernel, [shape(5, 128, 128), shape(256, 128)])(
            received, slot_row, slot_col, bottom, base_bottom
        )
        amounts = exchange(sent)
        start, back = find_loads(
            support, pattern, amounts, normals, phi_high, phi_low, base, couplings
        )
        image = applied(start, back, SHIFT)
        row = call(
            sums_kernel,
            shape(128, 128),
            [pltpu.VMEM((64, 128), F32), pltpu.VMEM((128, 128), F32)],
            scalars=1,
        )(
            pattern,
            start,
            image,
            forward(image),
            diagonal,
            couplings,
            tested,
            extra,
            own if count == 0 else jnp.zeros_like(own),
        )
        totals = exchange(row)
        solve = functools.partial(solve_kernel, count)
        if count == 0:
            outs = [shape(64, 128), shape(64, 128), shape(64, 128), shape(16, 128)]
            field, extra, last, memory = call(solve, outs)(
                totals, jnp.zeros((16, 128), F32), field, start, image, last, responses
            )
        else:
            outs = [shape(8, 3, 128), shape(8, 3, 128)]
            estimate, residual = call(solve, outs)(
                totals, memory, field, start, image, last, responses
            )
    new_state = lax.dynamic_update_slice(base_state, fresh[:, None], (0, 0, 0, 0))
    return (new_state, estimate, residual)


def solution(mesh):
    placed = (
        P(None, None, "fx", "fy"),
        P(("fx", "fy"), None, None),
        P(("fx", "fy"), None, None),
        P(("fx", "fy"), None),
        P(("fx", "fy"), None),
        P(("fx", "fy"), None, None),
        P(("fx", "fy"), None, None, None),
        P(("fx", "fy"), None),
        P(("fx", "fy"), None),
        P(("fx", "fy"), None, None),
        P(("fx", "fy"), None, None),
        P(None, ("fx", "fy"), None, None),
        P(None, ("fx", "fy"), None, None),
    )
    return jax.shard_map(
        on_device,
        mesh=mesh,
        in_specs=placed,
        out_specs=(
            P(None, None, "fx", "fy"),
            P(("fx", "fy"), None, None),
            P(("fx", "fy"), None, None),
        ),
        check_vma=False,
    )
```

```python
import functools

import jax
import jax.numpy as jnp
from jax import lax
from jax.experimental import pallas as pl
from jax.experimental.pallas import tpu as pltpu
from jax.sharding import PartitionSpec as P

AXES = ("fx", "fy")
DEVICES = 128
TOP_PRECISION = lax.Precision.HIGHEST
STEP_RATIO = 0.12
WALL_SPEED = 0.5
WALL_GAIN = 0.5
LOAD_SCALE = 4.0
PRESSURE_REF = 0.98
SHIFT = 1.25
PEERS = 4
F32 = jnp.float32
BF16 = jnp.bfloat16
VMEM = pltpu.VMEM
SMEM = pltpu.SMEM


def iota(shape, dim):
    return lax.broadcasted_iota(jnp.int32, shape, dim)


def edges_kernel(state, low_x, high_x, low_y, high_y):
    lanes = iota((128, 128), 1)
    first = jnp.zeros((128, 128), F32)
    final = jnp.zeros((128, 128), F32)
    for part in range(5):
        for z in range(8):
            line = part * 8 + z
            low_x[line : line + 1, :] = state[part, z, 0:1, :]
            high_x[line : line + 1, :] = state[part, z, 127:128, :]
            first = jnp.where(lanes == line, state[part, z, :, 0:1], first)
            final = jnp.where(lanes == line, state[part, z, :, 127:128], final)
    low_y[...] = first.T[:40]
    high_y[...] = final.T[:40]


def cell_terms(state):
    inverse = 1.0 / state[0]
    pressure = 0.4 * (
        state[4]
        - 0.5 * (state[1] * state[1] + state[2] * state[2] + state[3] * state[3]) * inverse
    )
    return inverse, pressure, jnp.sqrt(1.4 * pressure * inverse)


def flux_terms(state, terms, momentum):
    inverse, pressure, sound = terms
    velocity = state[momentum] * inverse
    flux = [part * velocity for part in state]
    flux[momentum] = flux[momentum] + pressure
    flux[4] = flux[4] + pressure * velocity
    return flux, jnp.abs(velocity) + sound


def face(left, right):
    (left_state, (left_flux, left_speed)), (right_state, (right_flux, right_speed)) = left, right
    half = 0.5 * jnp.maximum(left_speed, right_speed)
    return [
        0.5 * (left_flux[part] + right_flux[part])
        - half * (right_state[part] - left_state[part])
        for part in range(5)
    ]


def fluid_kernel(levels, state, low_x, high_x, low_y, high_y, *refs):
    base, sides = refs[-2:]
    lanes = iota((128, 128), 1)
    filler = jnp.zeros((88, 128), F32)
    low_cols = jnp.concatenate([low_y[...], filler], axis=0).T
    high_cols = jnp.concatenate([high_y[...], filler], axis=0).T
    for level, z in enumerate(levels):
        for part in range(5):
            line = part * 8 + z
            tile = state[part, z]
            sides[0, part] = jnp.concatenate([low_x[line : line + 1, :], tile[:127]], axis=0)
            sides[1, part] = jnp.concatenate([tile[1:], high_x[line : line + 1, :]], axis=0)
            sides[2, part] = jnp.where(
                lanes == 0, low_cols[:, line : line + 1], pltpu.roll(tile, 1, 1)
            )
            sides[3, part] = jnp.where(
                lanes == 127, high_cols[:, line : line + 1], pltpu.roll(tile, 127, 1)
            )

        def body(chunk, carry):
            rows = pl.ds(pl.multiple_of(chunk * 8, 8), 8)
            middle = [state[part, z, rows, :] for part in range(5)]
            own = cell_terms(middle)
            change = None
            for axis in range(2):
                here = (middle, flux_terms(middle, own, axis + 1))
                pair = []
                for side in range(2):
                    other = [sides[2 * axis + side, part, rows, :] for part in range(5)]
                    pair.append((other, flux_terms(other, cell_terms(other), axis + 1)))
                lower, upper = face(pair[0], here), face(here, pair[1])
                step = [upper[part] - lower[part] for part in range(5)]
                change = step if change is None else [x + y for x, y in zip(change, step)]
            here = (middle, flux_terms(middle, own, 3))
            if z < 7:
                other = [state[part, z + 1, rows, :] for part in range(5)]
                upper = face(here, (other, flux_terms(other, cell_terms(other), 3)))
            else:
                upper = here[1][0]
            if z > 0:
                other = [state[part, z - 1, rows, :] for part in range(5)]
                lower = face((other, flux_terms(other, cell_terms(other), 3)), here)
                upper = [x - y for x, y in zip(upper, lower)]
            for part in range(5):
                base[part, level, rows, :] = middle[part] - STEP_RATIO * (change[part] + upper[part])
            return carry

        lax.fori_loop(0, 16, body, 0)


def exact_dot(left, right):
    return jnp.dot(left, right, precision=TOP_PRECISION, preferred_element_type=F32)


def dot_nn(left, right):
    return lax.dot_general(left, right, (((1,), (0,)), ((), ())), preferred_element_type=F32)


def dot_nt(left, right):
    return lax.dot_general(left, right, (((1,), (1,)), ((), ())), preferred_element_type=F32)


def halves(value):
    high = value.astype(BF16)
    return high, (value - high.astype(F32)).astype(BF16)


def stacked_halves(value):
    high = value.astype(BF16).astype(F32)
    return jnp.concatenate([high, value - high], axis=0).astype(BF16)


def pack_kernel(own, points, normals, support, geo, slot_row, slot_col):
    across = jnp.broadcast_to(own[...].astype(F32), (128, 128))
    along = across.T
    same = across == along
    row_rank = jnp.sum(jnp.where(same & (iota((128, 128), 0) < iota((128, 128), 1)), 1.0, 0.0), axis=0, keepdims=True)
    col_rank = jnp.sum(jnp.where(same & (iota((128, 128), 1) < iota((128, 128), 0)), 1.0, 0.0), axis=1, keepdims=True)
    slots = 2.0 * along[:1] + row_rank
    slot_row[...] = jnp.broadcast_to(slots, (8, 128))
    slot_col[...] = 2.0 * across + col_rank
    ids = jnp.concatenate([support[...].astype(F32), jnp.zeros((128, 126), F32)], axis=1)
    values = [points[:, axis, :] for axis in range(3)]
    values += [normals[:, axis, :] for axis in range(3)]
    values = jnp.concatenate(values + [ids], axis=1)
    high = values.astype(BF16)
    rest = values - high.astype(F32)
    mid = rest.astype(BF16)
    low = (rest - mid.astype(F32)).astype(BF16)
    peers = iota((128, 128), 0).astype(F32)
    for rank in range(2):
        chosen = jnp.where(slots == 2.0 * peers + rank, 1.0, 0.0).astype(BF16)
        found = dot_nn(chosen, high) + dot_nn(chosen, mid) + dot_nn(chosen, low)
        for part in range(7):
            place = (3 * rank + part, 8 + 3 * rank + part - 3, 6 + rank)[
                0 if part < 3 else 1 if part < 6 else 2
            ]
            geo[pl.ds(place, 128, stride=16), :] = found[:, part * 128 : part * 128 + 128]
    for place in (14, 15):
        geo[pl.ds(place, 128, stride=16), :] = jnp.zeros((128, 128), F32)


def table_kernel(points, table):
    row = iota((8, 128), 0)
    zero = jnp.zeros((8, 128), F32)
    for block in range(8):
        tile = points[block] - 0.5
        size = jnp.broadcast_to(jnp.sum(tile * tile, axis=0, keepdims=True), (8, 128))
        size_high = size.astype(BF16).astype(F32)
        size_mid = (size - size_high).astype(BF16).astype(F32)
        size_low = size - size_high - size_mid
        sizes = jnp.where(
            row == 0, size_high, jnp.where(row == 1, size_mid, jnp.where(row == 2, size_low, 0.0))
        )
        for rank in range(2):
            pieces = [jnp.zeros((3, 128), F32)] * 2 + [jnp.zeros((2, 128), F32)]
            pieces[rank] = -2.0 * tile
            full = jnp.concatenate(pieces, axis=0) + jnp.where(row == 6 + rank, 1.0, 0.0)
            high = full.astype(BF16).astype(F32)
            mid = (full - high).astype(BF16).astype(F32)
            low = full - high - mid
            stack = jnp.concatenate(
                [high, mid, low, high, mid, high, sizes, zero] + [zero] * 8, axis=0
            )
            table[rank * 8 + block] = stack.T[:, :64].astype(BF16)


def spread_field(field, wide):
    for block in range(8):
        wide[block] = stacked_halves(field[pl.ds(block * 8, 8), :])


def moved_row(wide, tile, blocks, normal):
    left = jnp.concatenate([wide[block] for block in blocks], axis=1)
    moved = dot_nn(left, tile)
    moved = moved[:, :128] + moved[:, 128:]
    moved = moved[:3] + moved[8:11]
    return jnp.sum(moved * normal, axis=0, keepdims=True)


def tile_copy(source, target, sems, step):
    part = pl.ds(pl.multiple_of(step * 2 * PEERS, 2 * PEERS), 2 * PEERS)
    return pltpu.make_async_copy(source.at[part], target.at[part], sems.at[step])


def fetch_tiles(phi_hbm, phi, sems):
    def begin(step, carry):
        tile_copy(phi_hbm, phi, sems, step).start()
        return carry

    lax.fori_loop(0, STEPS, begin, 0)


def phi_kernel(support, geo, table, field, phi_hbm, motion, wide, phi, sems):
    spread_field(field, wide)
    row = iota((8, 128), 0)

    def body(step, carry):
        rows = []
        for peer in range(PEERS):
            start = pl.multiple_of((step * PEERS + peer) * 16, 16)
            tile = geo[pl.ds(start, 8), :] - 0.5
            normals = geo[pl.ds(start + 8, 8), :]
            square = tile * tile
            first = jnp.sum(jnp.where(row < 3, square, 0.0), axis=0, keepdims=True)
            second = jnp.sum(jnp.where((row >= 3) & (row < 6), square, 0.0), axis=0, keepdims=True)
            places = jnp.where(row < 6, tile, jnp.where(row == 6, first, second))
            high = places.astype(BF16).astype(F32)
            mid = (places - high).astype(BF16).astype(F32)
            low = places - high - mid
            ones = jnp.ones((8, 128), F32)
            right = jnp.concatenate(
                [high, high, high, mid, mid, low, ones, jnp.zeros((8, 128), F32)], axis=0
            ).astype(BF16)
            for rank in range(2):
                slot = (step * PEERS + peer) * 2 + rank
                tiles, blocks = [], []
                for k in range(2):
                    block = support[slot * 2 + k]
                    squared = jnp.maximum(dot_nn(table[rank * 8 + block], right), 1e-30)
                    ratio = squared * lax.rsqrt(squared)
                    reach = jnp.maximum(1.0 - ratio, 0.0)
                    reach = reach * reach
                    value = reach * reach * (4.0 * ratio + 1.0)
                    tiles.append(jnp.concatenate(halves(value), axis=1))
                    blocks.append(block)
                tile = jnp.concatenate(tiles, axis=0)
                phi[slot] = tile
                rows.append(moved_row(wide, tile, blocks, normals[3 * rank : 3 * rank + 3]))
        motion[pl.ds(pl.multiple_of(step * 2 * PEERS, 8), 8), :] = jnp.concatenate(rows, axis=0)
        tile_copy(phi, phi_hbm, sems, step).start()
        return carry

    lax.fori_loop(0, STEPS, body, 0)

    def finish(step, carry):
        tile_copy(phi, phi_hbm, sems, step).wait()
        return carry

    lax.fori_loop(0, STEPS, finish, 0)


def motion_kernel(support, geo, field, phi_hbm, motion, wide, phi, sems):
    fetch_tiles(phi_hbm, phi, sems)
    spread_field(field, wide)

    def body(step, carry):
        tile_copy(phi_hbm, phi, sems, step).wait()
        rows = []
        for index in range(2 * PEERS):
            slot = step * PEERS * 2 + index
            rank = index % 2
            start = pl.multiple_of((step * PEERS + index // 2) * 16, 16)
            normals = geo[pl.ds(start + 8, 8), :]
            blocks = [support[slot * 2 + k] for k in range(2)]
            rows.append(moved_row(wide, phi[slot], blocks, normals[3 * rank : 3 * rank + 3]))
        motion[pl.ds(pl.multiple_of(step * 2 * PEERS, 8), 8), :] = jnp.concatenate(rows, axis=0)
        return carry

    lax.fori_loop(0, STEPS, body, 0)


def wall_kernel(received, slot_row, slot_col, bottom, base, fresh, sent):
    lanes = iota((128, 256), 1).astype(F32)
    column = jnp.concatenate([slot_col[...], slot_col[...]], axis=1)
    argument = exact_dot(jnp.where(column == lanes, 1.0, 0.0), received[...])
    wall = WALL_SPEED * jnp.tanh(WALL_GAIN * argument)
    lower = [bottom[part] for part in range(5)]
    ghost = [lower[0], lower[1], lower[2], 2.0 * lower[0] * wall - lower[3], lower[4]]
    inverse = 1.0 / lower[0]

    def terms(state):
        velocity = state[3] * inverse
        pressure = 0.4 * (
            state[4]
            - 0.5 * (state[1] * state[1] + state[2] * state[2] + state[3] * state[3]) * inverse
        )
        flux = [part * velocity for part in state]
        flux[3] = flux[3] + pressure
        flux[4] = flux[4] + pressure * velocity
        return flux, jnp.abs(velocity) + jnp.sqrt(1.4 * pressure * inverse)

    ghost_flux, ghost_speed = terms(ghost)
    lower_flux, lower_speed = terms(lower)
    speed = jnp.maximum(ghost_speed, lower_speed)
    new = []
    for part in range(5):
        face = 0.5 * (ghost_flux[part] + lower_flux[part])
        if part == 3:
            face = face - 0.5 * speed * (lower[3] - ghost[3])
        new.append(base[part] + STEP_RATIO * face)
        fresh[part] = new[part]
    pressure = 0.4 * (
        new[4] - 0.5 * (new[1] * new[1] + new[2] * new[2] + new[3] * new[3]) / new[0]
    )
    amount = -LOAD_SCALE * (pressure - PRESSURE_REF)
    chosen = jnp.where(slot_row[:1] == iota((256, 128), 0).astype(F32), 1.0, 0.0)
    sent[...] = exact_dot(chosen, amount)


def spread_back(values, couplings, pattern, total):
    total[...] = jnp.zeros((64, 128), F32)

    def body(block, carry):
        stack = stacked_halves(values[pl.ds(pl.multiple_of(block * 8, 8), 8), :])
        for k in range(4):
            upper, lower = halves(couplings[block, k])
            term = dot_nn(stack, upper) + dot_nn(stack, lower)
            place = pl.ds(pl.multiple_of(pattern[block * 4 + k] * 8, 8), 8)
            total[place, :] = total[place, :] + term[:8] + term[8:]
        return carry

    lax.fori_loop(0, 8, body, 0)


def gather_forward(values, couplings, pattern, total):
    def body(block, carry):
        term = jnp.zeros((16, 128), F32)
        for k in range(4):
            place = pl.ds(pl.multiple_of(pattern[block * 4 + k] * 8, 8), 8)
            stack = stacked_halves(values[place, :])
            upper, lower = halves(couplings[block, k])
            term = term + dot_nt(stack, upper) + dot_nt(stack, lower)
        total[pl.ds(pl.multiple_of(block * 8, 8), 8), :] = term[:8] + term[8:]
        return carry

    lax.fori_loop(0, 8, body, 0)


def back_kernel(pattern, values, couplings, total):
    spread_back(values, couplings, pattern, total)


def loads_kernel(
    support, pattern, amounts, geo, phi_hbm, base, couplings, start, back, loads, phi, sems
):
    fetch_tiles(phi_hbm, phi, sems)
    loads[...] = jnp.zeros((8, 8, 128), F32)
    row = iota((8, 128), 0)

    def body(step, carry):
        tile_copy(phi_hbm, phi, sems, step).wait()
        forces = amounts[pl.ds(pl.multiple_of(step * 2 * PEERS, 8), 8), :]
        for peer in range(PEERS):
            place = pl.multiple_of((step * PEERS + peer) * 16, 16)
            tile = geo[pl.ds(place + 8, 8), :]
            for rank in range(2):
                index = peer * 2 + rank
                slot = step * PEERS * 2 + index
                kept = (row >= 3 * rank) & (row < 3 * rank + 3)
                stack = stacked_halves(jnp.where(kept, tile * forces[index : index + 1], 0.0))
                stack = jnp.concatenate([stack, stack], axis=1)
                term = dot_nt(stack, phi[slot])
                term = term[:8] + term[8:]
                for k in range(2):
                    block = support[slot * 2 + k]
                    loads[block] = loads[block] + term[:, k * 128 : k * 128 + 128]
        return carry

    lax.fori_loop(0, STEPS, body, 0)
    for block in range(8):
        tile = loads[block]
        start[pl.ds(block * 8, 8), :] = base[pl.ds(block * 8, 8), :] + jnp.where(
            row < 3, tile + pltpu.roll(tile, 5, 0), 0.0
        )
    spread_back(start, couplings, pattern, back)


def apply_kernel(shift, pattern, values, before, behind, diagonal, couplings, image, work):
    gather_forward(before, couplings, pattern, work)
    image[...] = (diagonal[...] - shift) * values[...] - (1.0 / 1024.0) * (
        work[...] + behind[...]
    )


def row_sum(value):
    return jnp.sum(value, axis=0, keepdims=True)


def sums_kernel(
    pattern, start, image, before, diagonal, couplings, tested, extra, own, row, work, stack
):
    gather_forward(before, couplings, pattern, work)
    first, second = start[...], image[...]
    stack[...] = jnp.zeros((128, 128), F32)
    for h in range(8):
        stack[pl.ds(h, 1), :] = row_sum(tested[h] * first)
        stack[pl.ds(8 + h, 1), :] = row_sum(tested[h] * second)
    third = second * ((diagonal[...] - SHIFT) * second - (2.0 / 1024.0) * work[...])
    stack[pl.ds(16, 1), :] = row_sum(first * first)
    stack[pl.ds(17, 1), :] = row_sum(first * second)
    stack[pl.ds(18, 1), :] = row_sum(second * second)
    stack[pl.ds(19, 1), :] = row_sum(third)
    stack[pl.ds(20, 1), :] = row_sum(extra[...] * first)
    stack[pl.ds(21, 1), :] = row_sum(extra[...] * second)
    sums = jnp.sum(stack[...], axis=1, keepdims=True)
    row[...] = jnp.broadcast_to(sums, (128, 128)).T + own[...]


def solve_kernel(
    count, received, memory, field, start, image, last, responses, estimate, residual, *more
):
    totals = row_sum(received[...])

    def lane(index):
        return totals[:, index : index + 1]

    lanes, row = iota((8, 128), 1), iota((8, 128), 0)

    def column(values):
        return jnp.sum(
            jnp.where(lanes == row, jnp.broadcast_to(values, (8, 128)), 0.0), axis=1, keepdims=True
        )

    m0, m1, m2, m3 = lane(16), lane(17), lane(18), lane(19)
    alpha = m0 / (m1 + SHIFT * m0)
    gain = 1.0 - alpha * SHIFT
    norm = gain * gain * m0 - 2.0 * gain * alpha * m1 + alpha * alpha * m2
    mix = gain + norm / m0
    curve = (
        mix * mix * (m1 + SHIFT * m0)
        - 2.0 * mix * alpha * (m2 + SHIFT * m1)
        + alpha * alpha * (m3 + SHIFT * m2)
    )
    follow = norm / curve
    c0 = alpha + follow * mix
    c1 = -follow * alpha
    change = c0 * start[...] + c1 * image[...]
    response = field[...] + change
    size = c0 * c0 * m0 + 2.0 * c0 * c1 * m1 + c1 * c1 * m2
    projected = c0 * totals + c1 * pltpu.roll(totals, 120, 1)
    lane_row = iota((1, 128), 1)
    if count == 0:
        picked = jnp.where(
            (lanes >= 64 + 8 * row) & (lanes < 72 + 8 * row),
            jnp.broadcast_to(totals, (8, 128)),
            0.0,
        )
        fold = jnp.where(
            (iota((128, 128), 0) >= 64) & (iota((128, 128), 0) % 8 == iota((128, 128), 1)), 1.0, 0.0
        )
        gram = exact_dot(picked, fold)
    else:
        overlap = c0 * lane(20) + c1 * lane(21)
        newest = size - overlap
        edge = projected - memory[8:9, :]
        edge = jnp.where(lane_row == 0, newest - overlap + memory[9:10, :1], edge)
        projected = jnp.where(lane_row == 0, newest, projected)
        gram = jnp.where(
            row == 0, jnp.broadcast_to(edge, (8, 128)), jnp.where(lanes == 0, column(edge), memory[:8, :])
        )
    system = jnp.where(lanes < 8, gram, jnp.where(lanes == 8, column(projected), 0.0))
    for j in range(8):
        pivot = system[j : j + 1] / system[j : j + 1, j : j + 1]
        system = jnp.where(row == j, pivot, system - system[:, j : j + 1] * pivot)
    result = response
    for h in range(8):
        weight = system[h : h + 1, 8:9]
        used = responses[h] if count == 0 or h > 0 else response - last[...]
        result = result - weight * used
    if count == 0:
        kept, saved = more
        estimate[...] = result
        residual[...] = change
        kept[...] = response
        saved[:8, :] = gram
        saved[8:16, :] = jnp.where(
            row == 0, jnp.broadcast_to(projected, (8, 128)), jnp.where(row == 1, size, 0.0)
        )
    else:
        for block in range(8):
            estimate[block] = result[block * 8 : block * 8 + 3]
            residual[block] = change[block * 8 : block * 8 + 3]


def shape(*dims, dtype=F32):
    return jax.ShapeDtypeStruct(dims, dtype)


def call(kernel, outs, scratch=(), scalars=0, cost=None, **kw):
    specs = [pl.BlockSpec(memory_space=SMEM)] * scalars

    def run(*args):
        return pl.pallas_call(
            kernel,
            out_shape=outs,
            in_specs=specs + [pl.BlockSpec()] * (len(args) - scalars),
            out_specs=jax.tree.map(lambda _: pl.BlockSpec(), outs),
            scratch_shapes=list(scratch),
            compiler_params=pltpu.CompilerParams(vmem_limit_bytes=14 << 20),
            cost_estimate=cost,
            **kw,
        )(*args)

    return run


def exchange(values):
    return lax.all_to_all(values, AXES, split_axis=0, concat_axis=0, tiled=True)


def forward(values):
    return lax.ppermute(values, AXES, [(i, (i + 1) % DEVICES) for i in range(DEVICES)])


def backward(values):
    return lax.ppermute(values, AXES, [((i + 1) % DEVICES, i) for i in range(DEVICES)])


def shift(values, axis, step):
    count = lax.axis_size(axis)
    return lax.ppermute(values, axis, [(i, (i + step) % count) for i in range(count)])


STEPS = DEVICES // PEERS
WIDE = pltpu.VMEM((8, 16, 128), BF16)
PHI_COST = pl.CostEstimate(flops=2_000_000_000, bytes_accessed=40_000_000, transcendentals=0)
RESIDENT = pl.BlockSpec(memory_space=pl.ANY)
HELD = [pltpu.VMEM((256, 256, 256), BF16), pltpu.SemaphoreType.DMA((DEVICES // PEERS,))]


def whole(kernel, scalars, in_specs, out_specs, outs, scratch, args):
    return pl.pallas_call(
        kernel,
        out_shape=outs,
        in_specs=[pl.BlockSpec(memory_space=SMEM)] * scalars + in_specs,
        out_specs=out_specs,
        scratch_shapes=scratch,
        compiler_params=pltpu.CompilerParams(vmem_limit_bytes=56 << 20),
        cost_estimate=PHI_COST,
    )(*args)


def build_phi(support, geo, table, field):
    return whole(
        phi_kernel,
        1,
        [pl.BlockSpec()] * 3,
        [RESIDENT, pl.BlockSpec()],
        [shape(256, 256, 256, dtype=BF16), shape(256, 128)],
        [WIDE] + HELD,
        (support, geo, table, field),
    )


def find_motion(support, geo, field, phi):
    return whole(
        motion_kernel,
        1,
        [pl.BlockSpec()] * 2 + [RESIDENT],
        pl.BlockSpec(),
        shape(256, 128),
        [WIDE] + HELD,
        (support, geo, field, phi),
    )


def find_loads(support, pattern, amounts, geo, phi, base, couplings):
    return whole(
        loads_kernel,
        2,
        [pl.BlockSpec()] * 2 + [RESIDENT] + [pl.BlockSpec()] * 2,
        [pl.BlockSpec(), pl.BlockSpec()],
        [shape(64, 128), shape(64, 128)],
        [pltpu.VMEM((8, 8, 128), F32)] + HELD,
        (support, pattern, amounts, geo, phi, base, couplings),
    )


def padded(values):
    wide = [(0, 0)] * (values.ndim - 2) + [(0, 5), (0, 0)]
    values = jnp.pad(values, wide)
    return values.reshape(values.shape[:-3] + (64, 128))


def on_device(
    fluid_state,
    surface_points,
    surface_normals,
    owner_ids,
    support_ids,
    struct_points,
    couplings,
    coupling_pattern,
    stiff_diagonal,
    struct_load,
    predicted,
    hist_residual,
    hist_response,
):
    pattern = coupling_pattern.reshape(32)
    geo, slot_row, slot_col = call(
        pack_kernel, [shape(2048, 128), shape(8, 128), shape(128, 128)]
    )(owner_ids, surface_points, surface_normals, support_ids)
    geo = exchange(geo)
    support = geo.reshape(128, 16, 128)[:, 6:8, :2].astype(jnp.int32).reshape(512)
    low_x, high_x, low_y, high_y = call(edges_kernel, [shape(40, 128)] * 4)(fluid_state)
    sides = [
        shift(low_x, "fx", -1),
        shift(high_x, "fx", 1),
        shift(low_y, "fy", -1),
        shift(high_y, "fy", 1),
    ]
    diagonal = padded(jnp.broadcast_to(stiff_diagonal[:, None, :], (8, 3, 128)))
    load = padded(struct_load)
    field = padded(predicted)
    tested = padded(hist_residual)
    responses = padded(hist_response)
    own = jnp.pad(
        jnp.einsum("hbdp,gbdp->hg", hist_residual, hist_residual, precision=TOP_PRECISION).reshape(
            1, 64
        ),
        ((0, 0), (64, 0)),
    )
    table = call(table_kernel, shape(16, 128, 64, dtype=BF16))(struct_points)

    def back_of(values):
        return call(back_kernel, shape(64, 128), scalars=1)(pattern, values, couplings)

    def applied(values, back, shift, gate=None):
        before, behind = forward(values), backward(back)
        if gate is not None:
            before, behind, _ = lax.optimization_barrier((before, behind, gate))
        return call(
            functools.partial(apply_kernel, shift),
            shape(64, 128),
            [pltpu.VMEM((64, 128), F32)],
            scalars=1,
        )(pattern, values, before, behind, diagonal, couplings)

    phi, motion = build_phi(support, geo, table, field)
    halos, motion = lax.optimization_barrier(
        ((sides[1], sides[0], sides[3], sides[2]), motion)
    )

    def fluid(levels, gate=None):
        ends = halos
        if gate is not None:
            ends, _ = lax.optimization_barrier((halos, gate))
        return call(
            functools.partial(fluid_kernel, levels),
            shape(5, len(levels), 128, 128),
            [pltpu.VMEM((4, 5, 128, 128), F32)],
            cost=pl.CostEstimate(
                flops=len(levels) * 40_000_000, bytes_accessed=len(levels) * 700_000, transcendentals=0
            ),
        )(fluid_state, *ends)

    bottom = fluid_state[:, 0]
    base_bottom = fluid((0,)).reshape(5, 128, 128)
    fluid_parts = []
    extra = field
    memory = diagonal
    last = field
    for count in range(2):
        if count > 0:
            motion = find_motion(support, geo, field, phi)
        received = exchange(motion)
        fresh, sent = call(wall_kernel, [shape(5, 128, 128), shape(256, 128)])(
            received, slot_row, slot_col, bottom, base_bottom
        )
        amounts = exchange(sent)
        base = load - applied(field, back_of(field), 0.0, sent)
        fluid_parts.append(fluid((1, 2, 3) if count == 0 else (6, 7), sent))
        amounts, fluid_parts[-1] = lax.optimization_barrier((amounts, fluid_parts[-1]))
        start, back = find_loads(support, pattern, amounts, geo, phi, base, couplings)
        image = applied(start, back, SHIFT)
        row = call(
            sums_kernel,
            shape(128, 128),
            [pltpu.VMEM((64, 128), F32), pltpu.VMEM((128, 128), F32)],
            scalars=1,
        )(
            pattern,
            start,
            image,
            forward(image),
            diagonal,
            couplings,
            tested,
            extra,
            own if count == 0 else jnp.zeros_like(own),
        )
        totals = exchange(row)
        if count == 0:
            fluid_parts.append(fluid((4, 5), row))
            totals, fluid_parts[-1] = lax.optimization_barrier((totals, fluid_parts[-1]))
        solve = functools.partial(solve_kernel, count)
        if count == 0:
            outs = [shape(64, 128), shape(64, 128), shape(64, 128), shape(16, 128)]
            field, extra, last, memory = call(solve, outs)(
                totals, jnp.zeros((16, 128), F32), field, start, image, last, responses
            )
        else:
            outs = [shape(8, 3, 128), shape(8, 3, 128)]
            estimate, residual = call(solve, outs)(
                totals, memory, field, start, image, last, responses
            )
    new_state = jnp.concatenate([fresh[:, None]] + fluid_parts, axis=1)
    return (new_state, estimate, residual)


def solution(mesh):
    placed = (
        P(None, None, "fx", "fy"),
        P(("fx", "fy"), None, None),
        P(("fx", "fy"), None, None),
        P(("fx", "fy"), None),
        P(("fx", "fy"), None),
        P(("fx", "fy"), None, None),
        P(("fx", "fy"), None, None, None),
        P(("fx", "fy"), None),
        P(("fx", "fy"), None),
        P(("fx", "fy"), None, None),
        P(("fx", "fy"), None, None),
        P(None, ("fx", "fy"), None, None),
        P(None, ("fx", "fy"), None, None),
    )
    return jax.shard_map(
        on_device,
        mesh=mesh,
        in_specs=placed,
        out_specs=(
            P(None, None, "fx", "fy"),
            P(("fx", "fy"), None, None),
            P(("fx", "fy"), None, None),
        ),
        check_vma=False,
    )
```

```python
import functools

import jax
import jax.numpy as jnp
from jax import lax
from jax.experimental import pallas as pl
from jax.experimental.pallas import tpu as pltpu
from jax.sharding import PartitionSpec as P

AXES = ("fx", "fy")
DEVICES = 128
TOP_PRECISION = lax.Precision.HIGHEST
STEP_RATIO = 0.12
WALL_SPEED = 0.5
WALL_GAIN = 0.5
LOAD_SCALE = 4.0
PRESSURE_REF = 0.98
SHIFT = 1.25
PEERS = 4
F32 = jnp.float32
BF16 = jnp.bfloat16
VMEM = pltpu.VMEM
SMEM = pltpu.SMEM


def iota(shape, dim):
    return lax.broadcasted_iota(jnp.int32, shape, dim)


def edges_kernel(state, low_x, high_x, low_y, high_y):
    lanes = iota((128, 128), 1)
    first = jnp.zeros((128, 128), F32)
    final = jnp.zeros((128, 128), F32)
    for part in range(5):
        for z in range(8):
            line = part * 8 + z
            low_x[line : line + 1, :] = state[part, z, 0:1, :]
            high_x[line : line + 1, :] = state[part, z, 127:128, :]
            first = jnp.where(lanes == line, state[part, z, :, 0:1], first)
            final = jnp.where(lanes == line, state[part, z, :, 127:128], final)
    low_y[...] = first.T[:40]
    high_y[...] = final.T[:40]


def cell_terms(state):
    inverse = 1.0 / state[0]
    pressure = 0.4 * (
        state[4]
        - 0.5 * (state[1] * state[1] + state[2] * state[2] + state[3] * state[3]) * inverse
    )
    return inverse, pressure, jnp.sqrt(1.4 * pressure * inverse)


def flux_terms(state, terms, momentum):
    inverse, pressure, sound = terms
    velocity = state[momentum] * inverse
    flux = [part * velocity for part in state]
    flux[momentum] = flux[momentum] + pressure
    flux[4] = flux[4] + pressure * velocity
    return flux, jnp.abs(velocity) + sound


def face(left, right):
    (left_state, (left_flux, left_speed)), (right_state, (right_flux, right_speed)) = left, right
    half = 0.5 * jnp.maximum(left_speed, right_speed)
    return [
        0.5 * (left_flux[part] + right_flux[part])
        - half * (right_state[part] - left_state[part])
        for part in range(5)
    ]


def fluid_kernel(levels, state, low_x, high_x, low_y, high_y, *refs):
    base, sides = refs[-2:]
    lanes = iota((128, 128), 1)
    filler = jnp.zeros((88, 128), F32)
    low_cols = jnp.concatenate([low_y[...], filler], axis=0).T
    high_cols = jnp.concatenate([high_y[...], filler], axis=0).T
    for level, z in enumerate(levels):
        for part in range(5):
            line = part * 8 + z
            tile = state[part, z]
            sides[0, part] = jnp.concatenate([low_x[line : line + 1, :], tile[:127]], axis=0)
            sides[1, part] = jnp.concatenate([tile[1:], high_x[line : line + 1, :]], axis=0)
            sides[2, part] = jnp.where(
                lanes == 0, low_cols[:, line : line + 1], pltpu.roll(tile, 1, 1)
            )
            sides[3, part] = jnp.where(
                lanes == 127, high_cols[:, line : line + 1], pltpu.roll(tile, 127, 1)
            )

        def body(chunk, carry):
            rows = pl.ds(pl.multiple_of(chunk * 8, 8), 8)
            middle = [state[part, z, rows, :] for part in range(5)]
            own = cell_terms(middle)
            change = None
            for axis in range(2):
                here = (middle, flux_terms(middle, own, axis + 1))
                pair = []
                for side in range(2):
                    other = [sides[2 * axis + side, part, rows, :] for part in range(5)]
                    pair.append((other, flux_terms(other, cell_terms(other), axis + 1)))
                lower, upper = face(pair[0], here), face(here, pair[1])
                step = [upper[part] - lower[part] for part in range(5)]
                change = step if change is None else [x + y for x, y in zip(change, step)]
            here = (middle, flux_terms(middle, own, 3))
            if z < 7:
                other = [state[part, z + 1, rows, :] for part in range(5)]
                upper = face(here, (other, flux_terms(other, cell_terms(other), 3)))
            else:
                upper = here[1][0]
            if z > 0:
                other = [state[part, z - 1, rows, :] for part in range(5)]
                lower = face((other, flux_terms(other, cell_terms(other), 3)), here)
                upper = [x - y for x, y in zip(upper, lower)]
            for part in range(5):
                base[part, level, rows, :] = middle[part] - STEP_RATIO * (change[part] + upper[part])
            return carry

        lax.fori_loop(0, 16, body, 0)


def exact_dot(left, right):
    return jnp.dot(left, right, precision=TOP_PRECISION, preferred_element_type=F32)


def dot_nn(left, right):
    return lax.dot_general(left, right, (((1,), (0,)), ((), ())), preferred_element_type=F32)


def dot_nt(left, right):
    return lax.dot_general(left, right, (((1,), (1,)), ((), ())), preferred_element_type=F32)


def halves(value):
    high = value.astype(BF16)
    return high, (value - high.astype(F32)).astype(BF16)


def stacked_halves(value):
    high = value.astype(BF16).astype(F32)
    return jnp.concatenate([high, value - high], axis=0).astype(BF16)


def pack_kernel(own, points, normals, support, geo, slot_row, slot_col):
    along = jnp.broadcast_to(own[...].astype(F32), (128, 128))
    across = along.T
    same = across == along
    row_rank = jnp.sum(jnp.where(same & (iota((128, 128), 0) < iota((128, 128), 1)), 1.0, 0.0), axis=0, keepdims=True)
    col_rank = jnp.sum(jnp.where(same & (iota((128, 128), 1) < iota((128, 128), 0)), 1.0, 0.0), axis=1, keepdims=True)
    slots = 2.0 * along[:1] + row_rank
    slot_row[...] = jnp.broadcast_to(slots, (8, 128))
    slot_col[...] = 2.0 * across + col_rank
    ids = jnp.concatenate([support[...].astype(F32), jnp.zeros((126, 128), F32)], axis=0).T
    values = [points[axis] for axis in range(3)] + [normals[axis] for axis in range(3)]
    values = jnp.concatenate(values + [ids], axis=1)
    high = values.astype(BF16)
    rest = values - high.astype(F32)
    mid = rest.astype(BF16)
    low = (rest - mid.astype(F32)).astype(BF16)
    peers = iota((128, 128), 0).astype(F32)
    for rank in range(2):
        chosen = jnp.where(slots == 2.0 * peers + rank, 1.0, 0.0).astype(BF16)
        found = dot_nn(chosen, high) + dot_nn(chosen, mid) + dot_nn(chosen, low)
        for part in range(7):
            place = (3 * rank + part, 8 + 3 * rank + part - 3, 6 + rank)[
                0 if part < 3 else 1 if part < 6 else 2
            ]
            geo[pl.ds(place, 128, stride=16), :] = found[:, part * 128 : part * 128 + 128]
    for place in (14, 15):
        geo[pl.ds(place, 128, stride=16), :] = jnp.zeros((128, 128), F32)


def table_kernel(points, table):
    row = iota((8, 128), 0)
    zero = jnp.zeros((8, 128), F32)
    for block in range(8):
        tile = points[:, block, :] - 0.5
        size = jnp.broadcast_to(jnp.sum(tile * tile, axis=0, keepdims=True), (8, 128))
        size_high = size.astype(BF16).astype(F32)
        size_mid = (size - size_high).astype(BF16).astype(F32)
        size_low = size - size_high - size_mid
        sizes = jnp.where(
            row == 0, size_high, jnp.where(row == 1, size_mid, jnp.where(row == 2, size_low, 0.0))
        )
        for rank in range(2):
            pieces = [jnp.zeros((3, 128), F32)] * 2 + [jnp.zeros((2, 128), F32)]
            pieces[rank] = -2.0 * tile
            full = jnp.concatenate(pieces, axis=0) + jnp.where(row == 6 + rank, 1.0, 0.0)
            high = full.astype(BF16).astype(F32)
            mid = (full - high).astype(BF16).astype(F32)
            low = full - high - mid
            stack = jnp.concatenate(
                [high, mid, low, high, mid, high, sizes, zero] + [zero] * 8, axis=0
            )
            table[rank * 8 + block] = stack.T[:, :64].astype(BF16)


def spread_field(field, wide):
    for block in range(8):
        wide[block] = stacked_halves(field[pl.ds(block * 8, 8), :])


def moved_row(wide, tile, blocks, normal):
    left = jnp.concatenate([wide[block] for block in blocks], axis=1)
    moved = dot_nn(left, tile)
    moved = moved[:, :128] + moved[:, 128:]
    moved = moved[:3] + moved[8:11]
    return jnp.sum(moved * normal, axis=0, keepdims=True)


def tile_copy(source, target, sems, step):
    part = pl.ds(pl.multiple_of(step * 2 * PEERS, 2 * PEERS), 2 * PEERS)
    return pltpu.make_async_copy(source.at[part], target.at[part], sems.at[step])


def fetch_tiles(phi_hbm, phi, sems):
    def begin(step, carry):
        tile_copy(phi_hbm, phi, sems, step).start()
        return carry

    lax.fori_loop(0, STEPS, begin, 0)


def phi_kernel(support, geo, table, field, phi_hbm, motion, wide, phi, sems):
    spread_field(field, wide)
    row = iota((8, 128), 0)

    def body(step, carry):
        rows = []
        for peer in range(PEERS):
            start = pl.multiple_of((step * PEERS + peer) * 16, 16)
            tile = geo[pl.ds(start, 8), :] - 0.5
            normals = geo[pl.ds(start + 8, 8), :]
            square = tile * tile
            first = jnp.sum(jnp.where(row < 3, square, 0.0), axis=0, keepdims=True)
            second = jnp.sum(jnp.where((row >= 3) & (row < 6), square, 0.0), axis=0, keepdims=True)
            places = jnp.where(row < 6, tile, jnp.where(row == 6, first, second))
            high = places.astype(BF16).astype(F32)
            mid = (places - high).astype(BF16).astype(F32)
            low = places - high - mid
            ones = jnp.ones((8, 128), F32)
            right = jnp.concatenate(
                [high, high, high, mid, mid, low, ones, jnp.zeros((8, 128), F32)], axis=0
            ).astype(BF16)
            for rank in range(2):
                slot = (step * PEERS + peer) * 2 + rank
                blocks = [support[slot * 2 + k] for k in range(2)]
                left = jnp.concatenate([table[rank * 8 + block] for block in blocks], axis=0)
                squared = jnp.maximum(dot_nn(left, right), 1e-30)
                ratio = squared * lax.rsqrt(squared)
                reach = jnp.maximum(1.0 - ratio, 0.0)
                reach = reach * reach
                value = reach * reach * (4.0 * ratio + 1.0)
                tile = jnp.concatenate(halves(value), axis=1)
                phi[slot] = tile
                rows.append(moved_row(wide, tile, blocks, normals[3 * rank : 3 * rank + 3]))
        motion[pl.ds(pl.multiple_of(step * 2 * PEERS, 8), 8), :] = jnp.concatenate(rows, axis=0)
        tile_copy(phi, phi_hbm, sems, step).start()
        return carry

    lax.fori_loop(0, STEPS, body, 0)

    def finish(step, carry):
        tile_copy(phi, phi_hbm, sems, step).wait()
        return carry

    lax.fori_loop(0, STEPS, finish, 0)


def basis_kernel(first, support, geo, field, start, image, responses, phi_hbm, motion, wide, phi, sems):
    def copy(step):
        there = pl.ds(pl.multiple_of((first + step) * 2 * PEERS, 2 * PEERS), 2 * PEERS)
        here = pl.ds(pl.multiple_of(step * 2 * PEERS, 2 * PEERS), 2 * PEERS)
        return pltpu.make_async_copy(phi_hbm.at[there], phi.at[here], sems.at[step])

    def begin(step, carry):
        copy(step).start()
        return carry

    lax.fori_loop(0, STEPS // 2, begin, 0)
    for block in range(8):
        pieces = []
        for axis in range(3):
            line = pl.ds(block * 8 + axis, 1)
            rows = [field[line, :], start[line, :], image[line, :]]
            rows += [responses[h, line, :] for h in range(8)]
            pieces.append(jnp.concatenate(rows + [jnp.zeros((5, 128), F32)], axis=0))
        wide[block] = stacked_halves(jnp.concatenate(pieces, axis=0))

    def body(step, carry):
        copy(step).wait()
        for index in range(2 * PEERS):
            here = step * PEERS * 2 + index
            slot = first * PEERS * 2 + here
            rank = index % 2
            place = pl.multiple_of(((first + step) * PEERS + index // 2) * 16, 16)
            normals = geo[pl.ds(place + 8, 8), :]
            left = jnp.concatenate([wide[support[slot * 2 + k]] for k in range(2)], axis=1)
            moved = dot_nn(left, phi[here])
            moved = moved[:, :128] + moved[:, 128:]
            moved = moved[:48] + moved[48:]
            total = moved[:16] * normals[3 * rank : 3 * rank + 1]
            for axis in range(1, 3):
                line = 3 * rank + axis
                total = total + moved[16 * axis : 16 * axis + 16] * normals[line : line + 1]
            motion[here] = total
        return carry

    lax.fori_loop(0, STEPS // 2, body, 0)


def wall_kernel(received, slot_row, slot_col, bottom, base, fresh, sent):
    lanes = iota((128, 256), 1).astype(F32)
    column = jnp.concatenate([slot_col[...], slot_col[...]], axis=1)
    argument = exact_dot(jnp.where(column == lanes, 1.0, 0.0), received[...])
    wall = WALL_SPEED * jnp.tanh(WALL_GAIN * argument)
    lower = [bottom[part] for part in range(5)]
    ghost = [lower[0], lower[1], lower[2], 2.0 * lower[0] * wall - lower[3], lower[4]]
    inverse = 1.0 / lower[0]

    def terms(state):
        velocity = state[3] * inverse
        pressure = 0.4 * (
            state[4]
            - 0.5 * (state[1] * state[1] + state[2] * state[2] + state[3] * state[3]) * inverse
        )
        flux = [part * velocity for part in state]
        flux[3] = flux[3] + pressure
        flux[4] = flux[4] + pressure * velocity
        return flux, jnp.abs(velocity) + jnp.sqrt(1.4 * pressure * inverse)

    ghost_flux, ghost_speed = terms(ghost)
    lower_flux, lower_speed = terms(lower)
    speed = jnp.maximum(ghost_speed, lower_speed)
    new = []
    for part in range(5):
        face = 0.5 * (ghost_flux[part] + lower_flux[part])
        if part == 3:
            face = face - 0.5 * speed * (lower[3] - ghost[3])
        new.append(base[part] + STEP_RATIO * face)
        fresh[part] = new[part]
    pressure = 0.4 * (
        new[4] - 0.5 * (new[1] * new[1] + new[2] * new[2] + new[3] * new[3]) / new[0]
    )
    amount = -LOAD_SCALE * (pressure - PRESSURE_REF)
    chosen = jnp.where(slot_row[:1] == iota((256, 128), 0).astype(F32), 1.0, 0.0)
    sent[...] = exact_dot(chosen, amount)


def spread_back(values, couplings, pattern, total):
    total[...] = jnp.zeros((64, 128), F32)

    def body(block, carry):
        stack = stacked_halves(values[pl.ds(pl.multiple_of(block * 8, 8), 8), :])
        for k in range(4):
            upper, lower = halves(couplings[block, k])
            term = dot_nn(stack, upper) + dot_nn(stack, lower)
            place = pl.ds(pl.multiple_of(pattern[block * 4 + k] * 8, 8), 8)
            total[place, :] = total[place, :] + term[:8] + term[8:]
        return carry

    lax.fori_loop(0, 8, body, 0)


def gather_forward(values, couplings, pattern, total):
    def body(block, carry):
        term = jnp.zeros((16, 128), F32)
        for k in range(4):
            place = pl.ds(pl.multiple_of(pattern[block * 4 + k] * 8, 8), 8)
            stack = stacked_halves(values[place, :])
            upper, lower = halves(couplings[block, k])
            term = term + dot_nt(stack, upper) + dot_nt(stack, lower)
        total[pl.ds(pl.multiple_of(block * 8, 8), 8), :] = term[:8] + term[8:]
        return carry

    lax.fori_loop(0, 8, body, 0)


def back_kernel(pattern, values, couplings, total):
    spread_back(values, couplings, pattern, total)


def loads_kernel(
    support, pattern, amounts, geo, phi_hbm, base, couplings, start, back, l0, l1, l2, l3, phi, sems
):
    fetch_tiles(phi_hbm, phi, sems)
    for loads in (l0, l1, l2, l3):
        loads[...] = jnp.zeros((8, 8, 128), F32)
    row = iota((8, 128), 0)

    def body(step, carry):
        tile_copy(phi_hbm, phi, sems, step).wait()
        forces = amounts[pl.ds(pl.multiple_of(step * 2 * PEERS, 8), 8), :]
        for peer in range(PEERS):
            place = pl.multiple_of((step * PEERS + peer) * 16, 16)
            tile = geo[pl.ds(place + 8, 8), :]
            for rank in range(2):
                index = peer * 2 + rank
                slot = step * PEERS * 2 + index
                kept = (row >= 3 * rank) & (row < 3 * rank + 3)
                stack = stacked_halves(jnp.where(kept, tile * forces[index : index + 1], 0.0))
                stack = jnp.concatenate([stack, stack], axis=1)
                term = dot_nt(stack, phi[slot])
                term = term[:8] + term[8:]
                for k in range(2):
                    block = support[slot * 2 + k]
                    loads = ((l0, l1), (l2, l3))[rank][k]
                    loads[block] = loads[block] + term[:, k * 128 : k * 128 + 128]
        return carry

    lax.fori_loop(0, STEPS, body, 0)
    for block in range(8):
        tile = (l0[block] + l1[block]) + (l2[block] + l3[block])
        start[pl.ds(block * 8, 8), :] = base[pl.ds(block * 8, 8), :] + jnp.where(
            row < 3, tile + pltpu.roll(tile, 5, 0), 0.0
        )
    spread_back(start, couplings, pattern, back)


def apply_kernel(shift, pattern, values, before, behind, diagonal, couplings, image, work):
    gather_forward(before, couplings, pattern, work)
    image[...] = (diagonal[...] - shift) * values[...] - (1.0 / 1024.0) * (
        work[...] + behind[...]
    )


def row_sum(value):
    return jnp.sum(value, axis=0, keepdims=True)


def sums_kernel(
    pattern, start, image, before, diagonal, couplings, tested, extra, own, row, work, stack
):
    gather_forward(before, couplings, pattern, work)
    first, second = start[...], image[...]
    stack[...] = jnp.zeros((128, 128), F32)
    for h in range(8):
        stack[pl.ds(h, 1), :] = row_sum(tested[h] * first)
        stack[pl.ds(8 + h, 1), :] = row_sum(tested[h] * second)
    third = second * ((diagonal[...] - SHIFT) * second - (2.0 / 1024.0) * work[...])
    stack[pl.ds(16, 1), :] = row_sum(first * first)
    stack[pl.ds(17, 1), :] = row_sum(first * second)
    stack[pl.ds(18, 1), :] = row_sum(second * second)
    stack[pl.ds(19, 1), :] = row_sum(third)
    stack[pl.ds(20, 1), :] = row_sum(extra[...] * first)
    stack[pl.ds(21, 1), :] = row_sum(extra[...] * second)
    sums = jnp.sum(stack[...], axis=1, keepdims=True)
    row[...] = jnp.broadcast_to(sums, (128, 128)).T + own[...]


def solve_kernel(
    count, received, memory, field, start, image, last, responses, *more
):
    if count == 0:
        halves_of, (estimate, residual, kept, saved, motion) = more[:2], more[2:]
    else:
        estimate, residual = more
    totals = row_sum(received[...])

    def lane(index):
        return totals[:, index : index + 1]

    lanes, row = iota((8, 128), 1), iota((8, 128), 0)

    def column(values):
        return jnp.sum(
            jnp.where(lanes == row, jnp.broadcast_to(values, (8, 128)), 0.0), axis=1, keepdims=True
        )

    m0, m1, m2, m3 = lane(16), lane(17), lane(18), lane(19)
    alpha = m0 / (m1 + SHIFT * m0)
    gain = 1.0 - alpha * SHIFT
    norm = gain * gain * m0 - 2.0 * gain * alpha * m1 + alpha * alpha * m2
    mix = gain + norm / m0
    curve = (
        mix * mix * (m1 + SHIFT * m0)
        - 2.0 * mix * alpha * (m2 + SHIFT * m1)
        + alpha * alpha * (m3 + SHIFT * m2)
    )
    follow = norm / curve
    c0 = alpha + follow * mix
    c1 = -follow * alpha
    change = c0 * start[...] + c1 * image[...]
    response = field[...] + change
    size = c0 * c0 * m0 + 2.0 * c0 * c1 * m1 + c1 * c1 * m2
    projected = c0 * totals + c1 * pltpu.roll(totals, 120, 1)
    lane_row = iota((1, 128), 1)
    if count == 0:
        picked = jnp.where(
            (lanes >= 64 + 8 * row) & (lanes < 72 + 8 * row),
            jnp.broadcast_to(totals, (8, 128)),
            0.0,
        )
        fold = jnp.where(
            (iota((128, 128), 0) >= 64) & (iota((128, 128), 0) % 8 == iota((128, 128), 1)), 1.0, 0.0
        )
        gram = exact_dot(picked, fold)
    else:
        overlap = c0 * lane(20) + c1 * lane(21)
        newest = size - overlap
        edge = projected - memory[8:9, :]
        edge = jnp.where(lane_row == 0, newest - overlap + memory[9:10, :1], edge)
        projected = jnp.where(lane_row == 0, newest, projected)
        gram = jnp.where(
            row == 0, jnp.broadcast_to(edge, (8, 128)), jnp.where(lanes == 0, column(edge), memory[:8, :])
        )
    system = jnp.where(lanes < 8, gram, jnp.where(lanes == 8, column(projected), 0.0))
    for j in range(8):
        pivot = system[j : j + 1] / system[j : j + 1, j : j + 1]
        system = jnp.where(row == j, pivot, system - system[:, j : j + 1] * pivot)
    result = response
    for h in range(8):
        weight = system[h : h + 1, 8:9]
        used = responses[h] if count == 0 or h > 0 else response - last[...]
        result = result - weight * used
    if count == 0:
        one = jnp.ones((1, 1), F32)
        mixture = jnp.concatenate(
            [one, c0, c1, -system[:, 8:9], jnp.zeros((5, 1), F32)], axis=0
        )
        mixture = jnp.broadcast_to(mixture, (16, 128))
        for half in range(2):
            for chunk in range(16):
                tiles = halves_of[half][chunk * 8 : chunk * 8 + 8]
                place = half * 128 + chunk * 8
                motion[place : place + 8, :] = jnp.sum(tiles * mixture[None], axis=1)
        estimate[...] = result
        residual[...] = change
        kept[...] = response
        saved[:8, :] = gram
        saved[8:16, :] = jnp.where(
            row == 0, jnp.broadcast_to(projected, (8, 128)), jnp.where(row == 1, size, 0.0)
        )
    else:
        for block in range(8):
            for axis in range(3):
                line = block * 8 + axis
                estimate[axis, block : block + 1, :] = result[line : line + 1]
                residual[axis, block : block + 1, :] = change[line : line + 1]


def shape(*dims, dtype=F32):
    return jax.ShapeDtypeStruct(dims, dtype)


def call(kernel, outs, scratch=(), scalars=0, cost=None, room=14, **kw):
    specs = [pl.BlockSpec(memory_space=SMEM)] * scalars

    def run(*args):
        return pl.pallas_call(
            kernel,
            out_shape=outs,
            in_specs=specs + [pl.BlockSpec()] * (len(args) - scalars),
            out_specs=jax.tree.map(lambda _: pl.BlockSpec(), outs),
            scratch_shapes=list(scratch),
            compiler_params=pltpu.CompilerParams(vmem_limit_bytes=room << 20),
            cost_estimate=cost,
            **kw,
        )(*args)

    return run


def exchange(values):
    return lax.all_to_all(values, AXES, split_axis=0, concat_axis=0, tiled=True)


def forward(values):
    return lax.ppermute(values, AXES, [(i, (i + 1) % DEVICES) for i in range(DEVICES)])


def backward(values):
    return lax.ppermute(values, AXES, [((i + 1) % DEVICES, i) for i in range(DEVICES)])


def shift(values, axis, step):
    count = lax.axis_size(axis)
    return lax.ppermute(values, axis, [(i, (i + step) % count) for i in range(count)])


STEPS = DEVICES // PEERS
WIDE = pltpu.VMEM((8, 16, 128), BF16)
PHI_COST = pl.CostEstimate(flops=2_000_000_000, bytes_accessed=40_000_000, transcendentals=0)
RESIDENT = pl.BlockSpec(memory_space=pl.ANY)
HELD = [pltpu.VMEM((256, 256, 256), BF16), pltpu.SemaphoreType.DMA((DEVICES // PEERS,))]


def whole(kernel, scalars, in_specs, out_specs, outs, scratch, args):
    return pl.pallas_call(
        kernel,
        out_shape=outs,
        in_specs=[pl.BlockSpec(memory_space=SMEM)] * scalars + in_specs,
        out_specs=out_specs,
        scratch_shapes=scratch,
        compiler_params=pltpu.CompilerParams(vmem_limit_bytes=56 << 20),
        cost_estimate=PHI_COST,
    )(*args)


def build_phi(support, geo, table, field):
    return whole(
        phi_kernel,
        1,
        [pl.BlockSpec()] * 3,
        [RESIDENT, pl.BlockSpec()],
        [shape(256, 256, 256, dtype=BF16), shape(256, 128)],
        [WIDE] + HELD,
        (support, geo, table, field),
    )


def basis_motion(half, support, geo, field, start, image, responses, phi):
    return whole(
        functools.partial(basis_kernel, half * STEPS // 2),
        1,
        [pl.BlockSpec()] * 5 + [RESIDENT],
        pl.BlockSpec(),
        shape(128, 16, 128),
        [
            pltpu.VMEM((8, 96, 128), BF16),
            pltpu.VMEM((128, 256, 256), BF16),
            pltpu.SemaphoreType.DMA((STEPS // 2,)),
        ],
        (support, geo, field, start, image, responses, phi),
    )


def find_loads(support, pattern, amounts, geo, phi, base, couplings):
    return whole(
        loads_kernel,
        2,
        [pl.BlockSpec()] * 2 + [RESIDENT] + [pl.BlockSpec()] * 2,
        [pl.BlockSpec(), pl.BlockSpec()],
        [shape(64, 128), shape(64, 128)],
        [pltpu.VMEM((8, 8, 128), F32)] * 4 + HELD,
        (support, pattern, amounts, geo, phi, base, couplings),
    )


def padded(values):
    wide = [(0, 0)] * (values.ndim - 2) + [(0, 5), (0, 0)]
    values = jnp.pad(values, wide)
    return values.reshape(values.shape[:-3] + (64, 128))


def on_device(
    fluid_state,
    surface_points,
    surface_normals,
    owner_ids,
    support_ids,
    struct_points,
    couplings,
    coupling_pattern,
    stiff_diagonal,
    struct_load,
    predicted,
    hist_residual,
    hist_response,
):
    pattern = coupling_pattern.reshape(32)
    geo, slot_row, slot_col = call(
        pack_kernel, [shape(2048, 128), shape(8, 128), shape(128, 128)], room=56
    )(
        owner_ids.T,
        jnp.transpose(surface_points, (1, 0, 2)),
        jnp.transpose(surface_normals, (1, 0, 2)),
        support_ids.T,
    )
    geo = exchange(geo)
    support = geo.reshape(128, 16, 128)[:, 6:8, :2].astype(jnp.int32).reshape(512)
    low_x, high_x, low_y, high_y = call(edges_kernel, [shape(40, 128)] * 4)(fluid_state)
    sides = [
        shift(low_x, "fx", -1),
        shift(high_x, "fx", 1),
        shift(low_y, "fy", -1),
        shift(high_y, "fy", 1),
    ]
    diagonal = padded(jnp.broadcast_to(stiff_diagonal[:, None, :], (8, 3, 128)))
    load = padded(struct_load)
    field = padded(predicted)
    tested = padded(hist_residual)
    responses = padded(hist_response)
    own = jnp.pad(
        jnp.einsum("hbdp,gbdp->hg", hist_residual, hist_residual, precision=TOP_PRECISION).reshape(
            1, 64
        ),
        ((0, 0), (64, 0)),
    )
    table = call(table_kernel, shape(16, 128, 64, dtype=BF16))(
        jnp.transpose(struct_points, (1, 0, 2))
    )

    def back_of(values):
        return call(back_kernel, shape(64, 128), scalars=1)(pattern, values, couplings)

    def applied(values, back, shift, gate=None):
        before, behind = forward(values), backward(back)
        if gate is not None:
            values = lax.optimization_barrier((values, gate))[0]
        return call(
            functools.partial(apply_kernel, shift),
            shape(64, 128),
            [pltpu.VMEM((64, 128), F32)],
            scalars=1,
        )(pattern, values, before, behind, diagonal, couplings)

    phi, motion = build_phi(support, geo, table, field)
    halos, motion = lax.optimization_barrier(
        ((sides[1], sides[0], sides[3], sides[2]), motion)
    )

    def fluid(levels, gate=None):
        ends = halos
        if gate is not None:
            ends, _ = lax.optimization_barrier((halos, gate))
        return call(
            functools.partial(fluid_kernel, levels),
            shape(5, len(levels), 128, 128),
            [pltpu.VMEM((4, 5, 128, 128), F32)],
            cost=pl.CostEstimate(
                flops=len(levels) * 40_000_000, bytes_accessed=len(levels) * 700_000, transcendentals=0
            ),
        )(fluid_state, *ends)

    bottom = fluid_state[:, 0]
    base_bottom = fluid((0,)).reshape(5, 128, 128)
    fluid_parts = []
    extra = field
    memory = diagonal
    last = field
    for count in range(2):
        received = exchange(motion)
        fresh, sent = call(wall_kernel, [shape(5, 128, 128), shape(256, 128)])(
            received, slot_row, slot_col, bottom, base_bottom
        )
        amounts = exchange(sent)
        ready = lax.optimization_barrier((field, motion))[0]
        stiff = applied(ready, back_of(ready), 0.0, sent)
        base = load - stiff
        fluid_parts.append(fluid((1, 2, 3) if count == 0 else (4,), sent))
        amounts, fluid_parts[-1] = lax.optimization_barrier((amounts, fluid_parts[-1]))
        start, back = find_loads(support, pattern, amounts, geo, phi, base, couplings)
        image = applied(start, back, SHIFT)
        ahead = forward(image)
        if count == 0:
            first_half = basis_motion(0, support, geo, field, start, image, responses, phi)
            ahead, first_half = lax.optimization_barrier((ahead, first_half))
        else:
            fluid_parts.append(fluid((5, 6, 7), image))
            ahead, fluid_parts[-1] = lax.optimization_barrier((ahead, fluid_parts[-1]))
        row = call(
            sums_kernel,
            shape(128, 128),
            [pltpu.VMEM((64, 128), F32), pltpu.VMEM((128, 128), F32)],
            scalars=1,
        )(
            pattern,
            start,
            image,
            ahead,
            diagonal,
            couplings,
            tested,
            extra,
            own if count == 0 else jnp.zeros_like(own),
        )
        totals = exchange(row)
        if count == 0:
            gated = lax.optimization_barrier((start, image, row))
            final_half = basis_motion(
                1, support, geo, field, gated[0], gated[1], responses, phi
            )
            totals, final_half = lax.optimization_barrier((totals, final_half))
        solve = functools.partial(solve_kernel, count)
        if count == 0:
            outs = [shape(64, 128)] * 3 + [shape(16, 128), shape(256, 128)]
            field, extra, last, memory, motion = call(solve, outs, room=56)(
                totals,
                jnp.zeros((16, 128), F32),
                field,
                start,
                image,
                last,
                responses,
                first_half,
                final_half,
            )
        else:
            outs = [shape(3, 8, 128), shape(3, 8, 128)]
            estimate, residual = call(solve, outs)(
                totals, memory, field, start, image, last, responses
            )
    new_state = jnp.concatenate([fresh[:, None]] + fluid_parts, axis=1)
    return (
        new_state,
        jnp.transpose(estimate, (1, 0, 2)),
        jnp.transpose(residual, (1, 0, 2)),
    )


def solution(mesh):
    placed = (
        P(None, None, "fx", "fy"),
        P(("fx", "fy"), None, None),
        P(("fx", "fy"), None, None),
        P(("fx", "fy"), None),
        P(("fx", "fy"), None),
        P(("fx", "fy"), None, None),
        P(("fx", "fy"), None, None, None),
        P(("fx", "fy"), None),
        P(("fx", "fy"), None),
        P(("fx", "fy"), None, None),
        P(("fx", "fy"), None, None),
        P(None, ("fx", "fy"), None, None),
        P(None, ("fx", "fy"), None, None),
    )
    return jax.shard_map(
        on_device,
        mesh=mesh,
        in_specs=placed,
        out_specs=(
            P(None, None, "fx", "fy"),
            P(("fx", "fy"), None, None),
            P(("fx", "fy"), None, None),
        ),
        check_vma=False,
    )
```

```python
import functools

import jax
import jax.numpy as jnp
from jax import lax
from jax.experimental import pallas as pl
from jax.experimental.pallas import tpu as pltpu
from jax.sharding import PartitionSpec as P

AXES = ("fx", "fy")
DEVICES = 128
TOP_PRECISION = lax.Precision.HIGHEST
STEP_RATIO = 0.12
WALL_SPEED = 0.5
WALL_GAIN = 0.5
LOAD_SCALE = 4.0
PRESSURE_REF = 0.98
SHIFT = 1.25
PEERS = 4
F32 = jnp.float32
BF16 = jnp.bfloat16
VMEM = pltpu.VMEM
SMEM = pltpu.SMEM


def iota(shape, dim):
    return lax.broadcasted_iota(jnp.int32, shape, dim)


def edges_kernel(state, low_x, high_x, low_y, high_y):
    lanes = iota((128, 128), 1)
    first = jnp.zeros((128, 128), F32)
    final = jnp.zeros((128, 128), F32)
    for part in range(5):
        for z in range(8):
            line = part * 8 + z
            low_x[line : line + 1, :] = state[part, z, 0:1, :]
            high_x[line : line + 1, :] = state[part, z, 127:128, :]
            first = jnp.where(lanes == line, state[part, z, :, 0:1], first)
            final = jnp.where(lanes == line, state[part, z, :, 127:128], final)
    low_y[...] = first.T[:40]
    high_y[...] = final.T[:40]


def cell_terms(state):
    inverse = 1.0 / state[0]
    pressure = 0.4 * (
        state[4]
        - 0.5 * (state[1] * state[1] + state[2] * state[2] + state[3] * state[3]) * inverse
    )
    return inverse, pressure, jnp.sqrt(1.4 * pressure * inverse)


def flux_terms(state, terms, momentum):
    inverse, pressure, sound = terms
    velocity = state[momentum] * inverse
    flux = [part * velocity for part in state]
    flux[momentum] = flux[momentum] + pressure
    flux[4] = flux[4] + pressure * velocity
    return flux, jnp.abs(velocity) + sound


def face(left, right):
    (left_state, (left_flux, left_speed)), (right_state, (right_flux, right_speed)) = left, right
    half = 0.5 * jnp.maximum(left_speed, right_speed)
    return [
        0.5 * (left_flux[part] + right_flux[part])
        - half * (right_state[part] - left_state[part])
        for part in range(5)
    ]


def fluid_kernel(levels, state, low_x, high_x, low_y, high_y, *refs):
    base, sides = refs[-2:]
    lanes = iota((128, 128), 1)
    filler = jnp.zeros((88, 128), F32)
    low_cols = jnp.concatenate([low_y[...], filler], axis=0).T
    high_cols = jnp.concatenate([high_y[...], filler], axis=0).T
    for level, z in enumerate(levels):
        for part in range(5):
            line = part * 8 + z
            tile = state[part, z]
            sides[0, part] = jnp.concatenate([low_x[line : line + 1, :], tile[:127]], axis=0)
            sides[1, part] = jnp.concatenate([tile[1:], high_x[line : line + 1, :]], axis=0)
            sides[2, part] = jnp.where(
                lanes == 0, low_cols[:, line : line + 1], pltpu.roll(tile, 1, 1)
            )
            sides[3, part] = jnp.where(
                lanes == 127, high_cols[:, line : line + 1], pltpu.roll(tile, 127, 1)
            )

        def body(chunk, carry):
            rows = pl.ds(pl.multiple_of(chunk * 8, 8), 8)
            middle = [state[part, z, rows, :] for part in range(5)]
            own = cell_terms(middle)
            change = None
            for axis in range(2):
                here = (middle, flux_terms(middle, own, axis + 1))
                pair = []
                for side in range(2):
                    other = [sides[2 * axis + side, part, rows, :] for part in range(5)]
                    pair.append((other, flux_terms(other, cell_terms(other), axis + 1)))
                lower, upper = face(pair[0], here), face(here, pair[1])
                step = [upper[part] - lower[part] for part in range(5)]
                change = step if change is None else [x + y for x, y in zip(change, step)]
            here = (middle, flux_terms(middle, own, 3))
            if z < 7:
                other = [state[part, z + 1, rows, :] for part in range(5)]
                upper = face(here, (other, flux_terms(other, cell_terms(other), 3)))
            else:
                upper = here[1][0]
            if z > 0:
                other = [state[part, z - 1, rows, :] for part in range(5)]
                lower = face((other, flux_terms(other, cell_terms(other), 3)), here)
                upper = [x - y for x, y in zip(upper, lower)]
            for part in range(5):
                base[part, level, rows, :] = middle[part] - STEP_RATIO * (change[part] + upper[part])
            return carry

        lax.fori_loop(0, 16, body, 0)


def exact_dot(left, right):
    return jnp.dot(left, right, precision=TOP_PRECISION, preferred_element_type=F32)


def dot_nn(left, right):
    return lax.dot_general(left, right, (((1,), (0,)), ((), ())), preferred_element_type=F32)


def dot_nt(left, right):
    return lax.dot_general(left, right, (((1,), (1,)), ((), ())), preferred_element_type=F32)


def halves(value):
    high = value.astype(BF16)
    return high, (value - high.astype(F32)).astype(BF16)


def stacked_halves(value):
    high = value.astype(BF16).astype(F32)
    return jnp.concatenate([high, value - high], axis=0).astype(BF16)


def pack_kernel(own, points, normals, support, geo, slot_row, slot_col):
    along = jnp.broadcast_to(own[...].astype(F32), (128, 128))
    across = along.T
    same = across == along
    row_rank = jnp.sum(jnp.where(same & (iota((128, 128), 0) < iota((128, 128), 1)), 1.0, 0.0), axis=0, keepdims=True)
    col_rank = jnp.sum(jnp.where(same & (iota((128, 128), 1) < iota((128, 128), 0)), 1.0, 0.0), axis=1, keepdims=True)
    slots = 2.0 * along[:1] + row_rank
    slot_row[...] = jnp.broadcast_to(slots, (8, 128))
    slot_col[...] = 2.0 * across + col_rank
    ids = jnp.concatenate([support[...].astype(F32), jnp.zeros((126, 128), F32)], axis=0).T
    values = [points[axis] for axis in range(3)] + [normals[axis] for axis in range(3)]
    values = jnp.concatenate(values + [ids], axis=1)
    high = values.astype(BF16)
    rest = values - high.astype(F32)
    mid = rest.astype(BF16)
    low = (rest - mid.astype(F32)).astype(BF16)
    peers = iota((128, 128), 0).astype(F32)
    for rank in range(2):
        chosen = jnp.where(slots == 2.0 * peers + rank, 1.0, 0.0).astype(BF16)
        found = dot_nn(chosen, high) + dot_nn(chosen, mid) + dot_nn(chosen, low)
        for part in range(7):
            place = (3 * rank + part, 8 + 3 * rank + part - 3, 6 + rank)[
                0 if part < 3 else 1 if part < 6 else 2
            ]
            geo[pl.ds(place, 128, stride=16), :] = found[:, part * 128 : part * 128 + 128]
    for place in (14, 15):
        geo[pl.ds(place, 128, stride=16), :] = jnp.zeros((128, 128), F32)


def table_kernel(points, table):
    row = iota((8, 128), 0)
    zero = jnp.zeros((8, 128), F32)
    for block in range(8):
        tile = points[:, block, :] - 0.5
        size = jnp.broadcast_to(jnp.sum(tile * tile, axis=0, keepdims=True), (8, 128))
        size_high = size.astype(BF16).astype(F32)
        size_mid = (size - size_high).astype(BF16).astype(F32)
        size_low = size - size_high - size_mid
        sizes = jnp.where(
            row == 0, size_high, jnp.where(row == 1, size_mid, jnp.where(row == 2, size_low, 0.0))
        )
        for rank in range(2):
            pieces = [jnp.zeros((3, 128), F32)] * 2 + [jnp.zeros((2, 128), F32)]
            pieces[rank] = -2.0 * tile
            full = jnp.concatenate(pieces, axis=0) + jnp.where(row == 6 + rank, 1.0, 0.0)
            high = full.astype(BF16).astype(F32)
            mid = (full - high).astype(BF16).astype(F32)
            low = full - high - mid
            stack = jnp.concatenate(
                [high, mid, low, high, mid, high, sizes, zero] + [zero] * 8, axis=0
            )
            table[rank * 8 + block] = stack.T[:, :64].astype(BF16)


def spread_field(field, wide):
    for block in range(8):
        wide[block] = stacked_halves(field[pl.ds(block * 8, 8), :])


def moved_row(wide, tile, blocks, normal):
    left = jnp.concatenate([wide[block] for block in blocks], axis=1)
    moved = dot_nn(left, tile)
    moved = moved[:, :128] + moved[:, 128:]
    moved = moved[:3] + moved[8:11]
    return jnp.sum(moved * normal, axis=0, keepdims=True)


def tile_copy(source, target, sems, step):
    part = pl.ds(pl.multiple_of(step * 2 * PEERS, 2 * PEERS), 2 * PEERS)
    return pltpu.make_async_copy(source.at[part], target.at[part], sems.at[step])


def fetch_tiles(phi_hbm, phi, sems):
    def begin(step, carry):
        tile_copy(phi_hbm, phi, sems, step).start()
        return carry

    lax.fori_loop(0, STEPS, begin, 0)


def phi_kernel(support, geo, table, field, phi_hbm, motion, wide, phi, sems):
    spread_field(field, wide)
    row = iota((8, 128), 0)

    def body(step, carry):
        rows = []
        for peer in range(PEERS):
            start = pl.multiple_of((step * PEERS + peer) * 16, 16)
            tile = geo[pl.ds(start, 8), :] - 0.5
            normals = geo[pl.ds(start + 8, 8), :]
            square = tile * tile
            first = jnp.sum(jnp.where(row < 3, square, 0.0), axis=0, keepdims=True)
            second = jnp.sum(jnp.where((row >= 3) & (row < 6), square, 0.0), axis=0, keepdims=True)
            places = jnp.where(row < 6, tile, jnp.where(row == 6, first, second))
            high = places.astype(BF16).astype(F32)
            mid = (places - high).astype(BF16).astype(F32)
            low = places - high - mid
            ones = jnp.ones((8, 128), F32)
            right = jnp.concatenate(
                [high, high, high, mid, mid, low, ones, jnp.zeros((8, 128), F32)], axis=0
            ).astype(BF16)
            for rank in range(2):
                slot = (step * PEERS + peer) * 2 + rank
                blocks = [support[slot * 2 + k] for k in range(2)]
                left = jnp.concatenate([table[rank * 8 + block] for block in blocks], axis=0)
                squared = jnp.maximum(dot_nn(left, right), 1e-30)
                ratio = squared * lax.rsqrt(squared)
                reach = jnp.maximum(1.0 - ratio, 0.0)
                reach = reach * reach
                value = reach * reach * (4.0 * ratio + 1.0)
                tile = jnp.concatenate(halves(value), axis=1)
                phi[slot] = tile
                rows.append(moved_row(wide, tile, blocks, normals[3 * rank : 3 * rank + 3]))
        motion[pl.ds(pl.multiple_of(step * 2 * PEERS, 8), 8), :] = jnp.concatenate(rows, axis=0)
        tile_copy(phi, phi_hbm, sems, step).start()
        return carry

    lax.fori_loop(0, STEPS, body, 0)

    def finish(step, carry):
        tile_copy(phi, phi_hbm, sems, step).wait()
        return carry

    lax.fori_loop(0, STEPS, finish, 0)


def basis_kernel(first, support, geo, field, start, image, responses, phi_hbm, motion, wide, phi, sems):
    def copy(step):
        there = pl.ds(pl.multiple_of((first + step) * 2 * PEERS, 2 * PEERS), 2 * PEERS)
        here = pl.ds(pl.multiple_of(step * 2 * PEERS, 2 * PEERS), 2 * PEERS)
        return pltpu.make_async_copy(phi_hbm.at[there], phi.at[here], sems.at[step])

    def begin(step, carry):
        copy(step).start()
        return carry

    lax.fori_loop(0, STEPS // 2, begin, 0)
    for block in range(8):
        pieces = []
        for axis in range(3):
            line = pl.ds(block * 8 + axis, 1)
            rows = [field[line, :], start[line, :], image[line, :]]
            rows += [responses[h, line, :] for h in range(8)]
            pieces.append(jnp.concatenate(rows + [jnp.zeros((5, 128), F32)], axis=0))
        wide[block] = stacked_halves(jnp.concatenate(pieces, axis=0))

    def body(step, carry):
        copy(step).wait()
        for index in range(2 * PEERS):
            here = step * PEERS * 2 + index
            slot = first * PEERS * 2 + here
            rank = index % 2
            place = pl.multiple_of(((first + step) * PEERS + index // 2) * 16, 16)
            normals = geo[pl.ds(place + 8, 8), :]
            left = jnp.concatenate([wide[support[slot * 2 + k]] for k in range(2)], axis=1)
            moved = dot_nn(left, phi[here])
            moved = moved[:, :128] + moved[:, 128:]
            moved = moved[:48] + moved[48:]
            total = moved[:16] * normals[3 * rank : 3 * rank + 1]
            for axis in range(1, 3):
                line = 3 * rank + axis
                total = total + moved[16 * axis : 16 * axis + 16] * normals[line : line + 1]
            motion[here] = total
        return carry

    lax.fori_loop(0, STEPS // 2, body, 0)


def wall_kernel(received, slot_row, slot_col, bottom, base, fresh, sent):
    lanes = iota((128, 256), 1).astype(F32)
    column = jnp.concatenate([slot_col[...], slot_col[...]], axis=1)
    argument = exact_dot(jnp.where(column == lanes, 1.0, 0.0), received[...])
    wall = WALL_SPEED * jnp.tanh(WALL_GAIN * argument)
    lower = [bottom[part] for part in range(5)]
    ghost = [lower[0], lower[1], lower[2], 2.0 * lower[0] * wall - lower[3], lower[4]]
    inverse = 1.0 / lower[0]

    def terms(state):
        velocity = state[3] * inverse
        pressure = 0.4 * (
            state[4]
            - 0.5 * (state[1] * state[1] + state[2] * state[2] + state[3] * state[3]) * inverse
        )
        flux = [part * velocity for part in state]
        flux[3] = flux[3] + pressure
        flux[4] = flux[4] + pressure * velocity
        return flux, jnp.abs(velocity) + jnp.sqrt(1.4 * pressure * inverse)

    ghost_flux, ghost_speed = terms(ghost)
    lower_flux, lower_speed = terms(lower)
    speed = jnp.maximum(ghost_speed, lower_speed)
    new = []
    for part in range(5):
        face = 0.5 * (ghost_flux[part] + lower_flux[part])
        if part == 3:
            face = face - 0.5 * speed * (lower[3] - ghost[3])
        new.append(base[part] + STEP_RATIO * face)
        fresh[part] = new[part]
    pressure = 0.4 * (
        new[4] - 0.5 * (new[1] * new[1] + new[2] * new[2] + new[3] * new[3]) / new[0]
    )
    amount = -LOAD_SCALE * (pressure - PRESSURE_REF)
    chosen = jnp.where(slot_row[:1] == iota((256, 128), 0).astype(F32), 1.0, 0.0)
    sent[...] = exact_dot(chosen, amount)


def spread_back(values, couplings, pattern, total):
    total[...] = jnp.zeros((64, 128), F32)

    def body(block, carry):
        stack = stacked_halves(values[pl.ds(pl.multiple_of(block * 8, 8), 8), :])
        for k in range(4):
            upper, lower = halves(couplings[block, k])
            term = dot_nn(stack, upper) + dot_nn(stack, lower)
            place = pl.ds(pl.multiple_of(pattern[block * 4 + k] * 8, 8), 8)
            total[place, :] = total[place, :] + term[:8] + term[8:]
        return carry

    lax.fori_loop(0, 8, body, 0)


def gather_forward(values, couplings, pattern, total):
    def body(block, carry):
        term = jnp.zeros((16, 128), F32)
        for k in range(4):
            place = pl.ds(pl.multiple_of(pattern[block * 4 + k] * 8, 8), 8)
            stack = stacked_halves(values[place, :])
            upper, lower = halves(couplings[block, k])
            term = term + dot_nt(stack, upper) + dot_nt(stack, lower)
        total[pl.ds(pl.multiple_of(block * 8, 8), 8), :] = term[:8] + term[8:]
        return carry

    lax.fori_loop(0, 8, body, 0)


def back_kernel(pattern, values, couplings, total):
    spread_back(values, couplings, pattern, total)


def loads_kernel(
    support, pattern, amounts, geo, phi_hbm, base, couplings, start, back, l0, l1, l2, l3, phi, sems
):
    fetch_tiles(phi_hbm, phi, sems)
    for loads in (l0, l1, l2, l3):
        loads[...] = jnp.zeros((8, 8, 128), F32)
    row = iota((8, 128), 0)

    def body(step, carry):
        tile_copy(phi_hbm, phi, sems, step).wait()
        forces = amounts[pl.ds(pl.multiple_of(step * 2 * PEERS, 8), 8), :]
        for peer in range(PEERS):
            place = pl.multiple_of((step * PEERS + peer) * 16, 16)
            tile = geo[pl.ds(place + 8, 8), :]
            for rank in range(2):
                index = peer * 2 + rank
                slot = step * PEERS * 2 + index
                kept = (row >= 3 * rank) & (row < 3 * rank + 3)
                stack = stacked_halves(jnp.where(kept, tile * forces[index : index + 1], 0.0))
                stack = jnp.concatenate([stack, stack], axis=1)
                term = dot_nt(stack, phi[slot])
                term = term[:8] + term[8:]
                for k in range(2):
                    block = support[slot * 2 + k]
                    loads = ((l0, l1), (l2, l3))[rank][k]
                    loads[block] = loads[block] + term[:, k * 128 : k * 128 + 128]
        return carry

    lax.fori_loop(0, STEPS, body, 0)
    for block in range(8):
        tile = (l0[block] + l1[block]) + (l2[block] + l3[block])
        start[pl.ds(block * 8, 8), :] = base[pl.ds(block * 8, 8), :] + jnp.where(
            row < 3, tile + pltpu.roll(tile, 5, 0), 0.0
        )
    spread_back(start, couplings, pattern, back)


def apply_kernel(shift, pattern, values, before, behind, diagonal, couplings, image, work):
    gather_forward(before, couplings, pattern, work)
    image[...] = (diagonal[...] - shift) * values[...] - (1.0 / 1024.0) * (
        work[...] + behind[...]
    )


def row_sum(value):
    return jnp.sum(value, axis=0, keepdims=True)


def sums_kernel(
    pattern, start, image, before, diagonal, couplings, tested, extra, own, row, work, stack
):
    gather_forward(before, couplings, pattern, work)
    first, second = start[...], image[...]
    stack[...] = jnp.zeros((128, 128), F32)
    for h in range(8):
        stack[pl.ds(h, 1), :] = row_sum(tested[h] * first)
        stack[pl.ds(8 + h, 1), :] = row_sum(tested[h] * second)
    third = second * ((diagonal[...] - SHIFT) * second - (2.0 / 1024.0) * work[...])
    stack[pl.ds(16, 1), :] = row_sum(first * first)
    stack[pl.ds(17, 1), :] = row_sum(first * second)
    stack[pl.ds(18, 1), :] = row_sum(second * second)
    stack[pl.ds(19, 1), :] = row_sum(third)
    stack[pl.ds(20, 1), :] = row_sum(extra[...] * first)
    stack[pl.ds(21, 1), :] = row_sum(extra[...] * second)
    sums = jnp.sum(stack[...], axis=1, keepdims=True)
    row[...] = jnp.broadcast_to(sums, (128, 128)).T + own[...]


def solve_kernel(
    count, received, memory, field, start, image, last, responses, *more
):
    if count == 0:
        halves_of, (estimate, residual, kept, saved, motion) = more[:2], more[2:]
    else:
        estimate, residual = more
    totals = row_sum(received[...])

    def lane(index):
        return totals[:, index : index + 1]

    lanes, row = iota((8, 128), 1), iota((8, 128), 0)

    def column(values):
        return jnp.sum(
            jnp.where(lanes == row, jnp.broadcast_to(values, (8, 128)), 0.0), axis=1, keepdims=True
        )

    m0, m1, m2, m3 = lane(16), lane(17), lane(18), lane(19)
    alpha = m0 / (m1 + SHIFT * m0)
    gain = 1.0 - alpha * SHIFT
    norm = gain * gain * m0 - 2.0 * gain * alpha * m1 + alpha * alpha * m2
    mix = gain + norm / m0
    curve = (
        mix * mix * (m1 + SHIFT * m0)
        - 2.0 * mix * alpha * (m2 + SHIFT * m1)
        + alpha * alpha * (m3 + SHIFT * m2)
    )
    follow = norm / curve
    c0 = alpha + follow * mix
    c1 = -follow * alpha
    change = c0 * start[...] + c1 * image[...]
    response = field[...] + change
    size = c0 * c0 * m0 + 2.0 * c0 * c1 * m1 + c1 * c1 * m2
    projected = c0 * totals + c1 * pltpu.roll(totals, 120, 1)
    lane_row = iota((1, 128), 1)
    if count == 0:
        picked = jnp.where(
            (lanes >= 64 + 8 * row) & (lanes < 72 + 8 * row),
            jnp.broadcast_to(totals, (8, 128)),
            0.0,
        )
        fold = jnp.where(
            (iota((128, 128), 0) >= 64) & (iota((128, 128), 0) % 8 == iota((128, 128), 1)), 1.0, 0.0
        )
        gram = exact_dot(picked, fold)
    else:
        overlap = c0 * lane(20) + c1 * lane(21)
        newest = size - overlap
        edge = projected - memory[8:9, :]
        edge = jnp.where(lane_row == 0, newest - overlap + memory[9:10, :1], edge)
        projected = jnp.where(lane_row == 0, newest, projected)
        gram = jnp.where(
            row == 0, jnp.broadcast_to(edge, (8, 128)), jnp.where(lanes == 0, column(edge), memory[:8, :])
        )
    system = jnp.where(lanes < 8, gram, jnp.where(lanes == 8, column(projected), 0.0))
    for j in range(8):
        pivot = system[j : j + 1] / system[j : j + 1, j : j + 1]
        system = jnp.where(row == j, pivot, system - system[:, j : j + 1] * pivot)
    result = response
    for h in range(8):
        weight = system[h : h + 1, 8:9]
        used = responses[h] if count == 0 or h > 0 else response - last[...]
        result = result - weight * used
    if count == 0:
        one = jnp.ones((1, 1), F32)
        mixture = jnp.concatenate(
            [one, c0, c1, -system[:, 8:9], jnp.zeros((5, 1), F32)], axis=0
        )
        mixture = jnp.broadcast_to(mixture, (16, 128))
        for half in range(2):
            for chunk in range(16):
                tiles = halves_of[half][chunk * 8 : chunk * 8 + 8]
                place = half * 128 + chunk * 8
                motion[place : place + 8, :] = jnp.sum(tiles * mixture[None], axis=1)
        estimate[...] = result
        residual[...] = change
        kept[...] = response
        saved[:8, :] = gram
        saved[8:16, :] = jnp.where(
            row == 0, jnp.broadcast_to(projected, (8, 128)), jnp.where(row == 1, size, 0.0)
        )
    else:
        for block in range(8):
            for axis in range(3):
                line = block * 8 + axis
                estimate[axis, block : block + 1, :] = result[line : line + 1]
                residual[axis, block : block + 1, :] = change[line : line + 1]


def shape(*dims, dtype=F32):
    return jax.ShapeDtypeStruct(dims, dtype)


def call(kernel, outs, scratch=(), scalars=0, cost=None, room=14, **kw):
    specs = [pl.BlockSpec(memory_space=SMEM)] * scalars

    def run(*args):
        return pl.pallas_call(
            kernel,
            out_shape=outs,
            in_specs=specs + [pl.BlockSpec()] * (len(args) - scalars),
            out_specs=jax.tree.map(lambda _: pl.BlockSpec(), outs),
            scratch_shapes=list(scratch),
            compiler_params=pltpu.CompilerParams(vmem_limit_bytes=room << 20),
            cost_estimate=cost,
            **kw,
        )(*args)

    return run


def exchange(values):
    return lax.all_to_all(values, AXES, split_axis=0, concat_axis=0, tiled=True)


def forward(values):
    return lax.ppermute(values, AXES, [(i, (i + 1) % DEVICES) for i in range(DEVICES)])


def backward(values):
    return lax.ppermute(values, AXES, [((i + 1) % DEVICES, i) for i in range(DEVICES)])


def shift(values, axis, step):
    count = lax.axis_size(axis)
    return lax.ppermute(values, axis, [(i, (i + step) % count) for i in range(count)])


STEPS = DEVICES // PEERS
WIDE = pltpu.VMEM((8, 16, 128), BF16)
PHI_COST = pl.CostEstimate(flops=2_000_000_000, bytes_accessed=40_000_000, transcendentals=0)
RESIDENT = pl.BlockSpec(memory_space=pl.ANY)
HELD = [pltpu.VMEM((256, 256, 256), BF16), pltpu.SemaphoreType.DMA((DEVICES // PEERS,))]


def whole(kernel, scalars, in_specs, out_specs, outs, scratch, args):
    return pl.pallas_call(
        kernel,
        out_shape=outs,
        in_specs=[pl.BlockSpec(memory_space=SMEM)] * scalars + in_specs,
        out_specs=out_specs,
        scratch_shapes=scratch,
        compiler_params=pltpu.CompilerParams(vmem_limit_bytes=56 << 20),
        cost_estimate=PHI_COST,
    )(*args)


def build_phi(support, geo, table, field):
    return whole(
        phi_kernel,
        1,
        [pl.BlockSpec()] * 3,
        [RESIDENT, pl.BlockSpec()],
        [shape(256, 256, 256, dtype=BF16), shape(256, 128)],
        [WIDE] + HELD,
        (support, geo, table, field),
    )


def basis_motion(half, support, geo, field, start, image, responses, phi):
    return whole(
        functools.partial(basis_kernel, half * STEPS // 2),
        1,
        [pl.BlockSpec()] * 5 + [RESIDENT],
        pl.BlockSpec(),
        shape(128, 16, 128),
        [
            pltpu.VMEM((8, 96, 128), BF16),
            pltpu.VMEM((128, 256, 256), BF16),
            pltpu.SemaphoreType.DMA((STEPS // 2,)),
        ],
        (support, geo, field, start, image, responses, phi),
    )


def find_loads(support, pattern, amounts, geo, phi, base, couplings):
    return whole(
        loads_kernel,
        2,
        [pl.BlockSpec()] * 2 + [RESIDENT] + [pl.BlockSpec()] * 2,
        [pl.BlockSpec(), pl.BlockSpec()],
        [shape(64, 128), shape(64, 128)],
        [pltpu.VMEM((8, 8, 128), F32)] * 4 + HELD,
        (support, pattern, amounts, geo, phi, base, couplings),
    )


def padded(values):
    wide = [(0, 0)] * (values.ndim - 2) + [(0, 5), (0, 0)]
    values = jnp.pad(values, wide)
    return values.reshape(values.shape[:-3] + (64, 128))


def on_device(
    fluid_state,
    surface_points,
    surface_normals,
    owner_ids,
    support_ids,
    struct_points,
    couplings,
    coupling_pattern,
    stiff_diagonal,
    struct_load,
    predicted,
    hist_residual,
    hist_response,
):
    pattern = coupling_pattern.reshape(32)
    geo, slot_row, slot_col = call(
        pack_kernel, [shape(2048, 128), shape(8, 128), shape(128, 128)], room=56
    )(
        owner_ids.T,
        jnp.transpose(surface_points, (1, 0, 2)),
        jnp.transpose(surface_normals, (1, 0, 2)),
        support_ids.T,
    )
    geo = exchange(geo)
    support = geo.reshape(128, 16, 128)[:, 6:8, :2].astype(jnp.int32).reshape(512)
    low_x, high_x, low_y, high_y = call(edges_kernel, [shape(40, 128)] * 4)(fluid_state)
    sides = [
        shift(low_x, "fx", -1),
        shift(high_x, "fx", 1),
        shift(low_y, "fy", -1),
        shift(high_y, "fy", 1),
    ]
    diagonal = padded(jnp.broadcast_to(stiff_diagonal[:, None, :], (8, 3, 128)))
    load = padded(struct_load)
    field = padded(predicted)
    tested = padded(hist_residual)
    responses = padded(hist_response)
    own = jnp.pad(
        jnp.einsum("hbdp,gbdp->hg", hist_residual, hist_residual, precision=TOP_PRECISION).reshape(
            1, 64
        ),
        ((0, 0), (64, 0)),
    )
    table = call(table_kernel, shape(16, 128, 64, dtype=BF16))(
        jnp.transpose(struct_points, (1, 0, 2))
    )

    def back_of(values):
        return call(back_kernel, shape(64, 128), scalars=1)(pattern, values, couplings)

    def applied(values, back, shift, gate=None):
        before = forward(values)
        if gate is not None:
            back, before = lax.optimization_barrier((back, before))
            values = lax.optimization_barrier((values, gate))[0]
        behind = backward(back)
        return call(
            functools.partial(apply_kernel, shift),
            shape(64, 128),
            [pltpu.VMEM((64, 128), F32)],
            scalars=1,
        )(pattern, values, before, behind, diagonal, couplings)

    phi, motion = build_phi(support, geo, table, field)
    halos, motion = lax.optimization_barrier(
        ((sides[1], sides[0], sides[3], sides[2]), motion)
    )

    def fluid(levels, gate=None):
        ends = halos
        if gate is not None:
            ends, _ = lax.optimization_barrier((halos, gate))
        return call(
            functools.partial(fluid_kernel, levels),
            shape(5, len(levels), 128, 128),
            [pltpu.VMEM((4, 5, 128, 128), F32)],
            cost=pl.CostEstimate(
                flops=len(levels) * 40_000_000, bytes_accessed=len(levels) * 700_000, transcendentals=0
            ),
        )(fluid_state, *ends)

    bottom = fluid_state[:, 0]
    base_bottom = fluid((0,)).reshape(5, 128, 128)
    fluid_parts = []
    extra = field
    memory = diagonal
    last = field
    for count in range(2):
        received = exchange(motion)
        fresh, sent = call(wall_kernel, [shape(5, 128, 128), shape(256, 128)])(
            received, slot_row, slot_col, bottom, base_bottom
        )
        amounts = exchange(sent)
        ready = lax.optimization_barrier((field, motion))[0]
        stiff = applied(ready, back_of(ready), 0.0, sent)
        base = load - stiff
        start, back = find_loads(support, pattern, amounts, geo, phi, base, couplings)
        image = applied(start, back, SHIFT)
        ahead = forward(image)
        if count == 0:
            first_half = basis_motion(0, support, geo, field, start, image, responses, phi)
            ahead, first_half = lax.optimization_barrier((ahead, first_half))
        else:
            fluid_parts.append(fluid((4, 5, 6, 7), image))
            ahead, fluid_parts[-1] = lax.optimization_barrier((ahead, fluid_parts[-1]))
        row = call(
            sums_kernel,
            shape(128, 128),
            [pltpu.VMEM((64, 128), F32), pltpu.VMEM((128, 128), F32)],
            scalars=1,
        )(
            pattern,
            start,
            image,
            ahead,
            diagonal,
            couplings,
            tested,
            extra,
            own if count == 0 else jnp.zeros_like(own),
        )
        totals = exchange(row)
        if count == 0:
            gated = lax.optimization_barrier((start, image, row))
            final_half = basis_motion(
                1, support, geo, field, gated[0], gated[1], responses, phi
            )
            totals, final_half = lax.optimization_barrier((totals, final_half))
        else:
            fluid_parts.insert(0, fluid((1, 2, 3), row))
            totals, fluid_parts[0] = lax.optimization_barrier((totals, fluid_parts[0]))
        solve = functools.partial(solve_kernel, count)
        if count == 0:
            outs = [shape(64, 128)] * 3 + [shape(16, 128), shape(256, 128)]
            field, extra, last, memory, motion = call(solve, outs, room=56)(
                totals,
                jnp.zeros((16, 128), F32),
                field,
                start,
                image,
                last,
                responses,
                first_half,
                final_half,
            )
        else:
            outs = [shape(3, 8, 128), shape(3, 8, 128)]
            estimate, residual = call(solve, outs)(
                totals, memory, field, start, image, last, responses
            )
    new_state = jnp.concatenate([fresh[:, None]] + fluid_parts, axis=1)
    return (
        new_state,
        jnp.transpose(estimate, (1, 0, 2)),
        jnp.transpose(residual, (1, 0, 2)),
    )


def solution(mesh):
    placed = (
        P(None, None, "fx", "fy"),
        P(("fx", "fy"), None, None),
        P(("fx", "fy"), None, None),
        P(("fx", "fy"), None),
        P(("fx", "fy"), None),
        P(("fx", "fy"), None, None),
        P(("fx", "fy"), None, None, None),
        P(("fx", "fy"), None),
        P(("fx", "fy"), None),
        P(("fx", "fy"), None, None),
        P(("fx", "fy"), None, None),
        P(None, ("fx", "fy"), None, None),
        P(None, ("fx", "fy"), None, None),
    )
    return jax.shard_map(
        on_device,
        mesh=mesh,
        in_specs=placed,
        out_specs=(
            P(None, None, "fx", "fy"),
            P(("fx", "fy"), None, None),
            P(("fx", "fy"), None, None),
        ),
        check_vma=False,
    )
```

```python
import functools

import jax
import jax.numpy as jnp
from jax import lax
from jax.experimental import pallas as pl
from jax.experimental.pallas import tpu as pltpu
from jax.sharding import PartitionSpec as P

AXES = ("fx", "fy")
DEVICES = 128
TOP_PRECISION = lax.Precision.HIGHEST
STEP_RATIO = 0.12
WALL_SPEED = 0.5
WALL_GAIN = 0.5
LOAD_SCALE = 4.0
PRESSURE_REF = 0.98
SHIFT = 1.25
PEERS = 4
F32 = jnp.float32
BF16 = jnp.bfloat16
VMEM = pltpu.VMEM
SMEM = pltpu.SMEM


def iota(shape, dim):
    return lax.broadcasted_iota(jnp.int32, shape, dim)


def edges_kernel(state, low_x, high_x, low_y, high_y):
    lanes = iota((128, 128), 1)
    first = jnp.zeros((128, 128), F32)
    final = jnp.zeros((128, 128), F32)
    for part in range(5):
        for z in range(8):
            line = part * 8 + z
            low_x[line : line + 1, :] = state[part, z, 0:1, :]
            high_x[line : line + 1, :] = state[part, z, 127:128, :]
            first = jnp.where(lanes == line, state[part, z, :, 0:1], first)
            final = jnp.where(lanes == line, state[part, z, :, 127:128], final)
    low_y[...] = first.T[:40]
    high_y[...] = final.T[:40]


def cell_terms(state):
    inverse = 1.0 / state[0]
    pressure = 0.4 * (
        state[4]
        - 0.5 * (state[1] * state[1] + state[2] * state[2] + state[3] * state[3]) * inverse
    )
    return inverse, pressure, jnp.sqrt(1.4 * pressure * inverse)


def flux_terms(state, terms, momentum):
    inverse, pressure, sound = terms
    velocity = state[momentum] * inverse
    flux = [part * velocity for part in state]
    flux[momentum] = flux[momentum] + pressure
    flux[4] = flux[4] + pressure * velocity
    return flux, jnp.abs(velocity) + sound


def face(left, right):
    (left_state, (left_flux, left_speed)), (right_state, (right_flux, right_speed)) = left, right
    half = 0.5 * jnp.maximum(left_speed, right_speed)
    return [
        0.5 * (left_flux[part] + right_flux[part])
        - half * (right_state[part] - left_state[part])
        for part in range(5)
    ]


def fluid_kernel(levels, state, low_x, high_x, low_y, high_y, *refs):
    base, sides = refs[-2:]
    lanes = iota((128, 128), 1)
    filler = jnp.zeros((88, 128), F32)
    low_cols = jnp.concatenate([low_y[...], filler], axis=0).T
    high_cols = jnp.concatenate([high_y[...], filler], axis=0).T
    for level, z in enumerate(levels):
        for part in range(5):
            line = part * 8 + z
            tile = state[part, z]
            sides[0, part] = jnp.concatenate([low_x[line : line + 1, :], tile[:127]], axis=0)
            sides[1, part] = jnp.concatenate([tile[1:], high_x[line : line + 1, :]], axis=0)
            sides[2, part] = jnp.where(
                lanes == 0, low_cols[:, line : line + 1], pltpu.roll(tile, 1, 1)
            )
            sides[3, part] = jnp.where(
                lanes == 127, high_cols[:, line : line + 1], pltpu.roll(tile, 127, 1)
            )

        def body(chunk, carry):
            rows = pl.ds(pl.multiple_of(chunk * 8, 8), 8)
            middle = [state[part, z, rows, :] for part in range(5)]
            own = cell_terms(middle)
            change = None
            for axis in range(2):
                here = (middle, flux_terms(middle, own, axis + 1))
                pair = []
                for side in range(2):
                    other = [sides[2 * axis + side, part, rows, :] for part in range(5)]
                    pair.append((other, flux_terms(other, cell_terms(other), axis + 1)))
                lower, upper = face(pair[0], here), face(here, pair[1])
                step = [upper[part] - lower[part] for part in range(5)]
                change = step if change is None else [x + y for x, y in zip(change, step)]
            here = (middle, flux_terms(middle, own, 3))
            if z < 7:
                other = [state[part, z + 1, rows, :] for part in range(5)]
                upper = face(here, (other, flux_terms(other, cell_terms(other), 3)))
            else:
                upper = here[1][0]
            if z > 0:
                other = [state[part, z - 1, rows, :] for part in range(5)]
                lower = face((other, flux_terms(other, cell_terms(other), 3)), here)
                upper = [x - y for x, y in zip(upper, lower)]
            for part in range(5):
                base[part, level, rows, :] = middle[part] - STEP_RATIO * (change[part] + upper[part])
            return carry

        lax.fori_loop(0, 16, body, 0)


def exact_dot(left, right):
    return jnp.dot(left, right, precision=TOP_PRECISION, preferred_element_type=F32)


def dot_nn(left, right):
    return lax.dot_general(left, right, (((1,), (0,)), ((), ())), preferred_element_type=F32)


def dot_nt(left, right):
    return lax.dot_general(left, right, (((1,), (1,)), ((), ())), preferred_element_type=F32)


def halves(value):
    high = value.astype(BF16)
    return high, (value - high.astype(F32)).astype(BF16)


def stacked_halves(value):
    high = value.astype(BF16).astype(F32)
    return jnp.concatenate([high, value - high], axis=0).astype(BF16)


def pack_kernel(own, points, normals, support, geo, slot_row, slot_col):
    along = jnp.broadcast_to(own[...].astype(F32), (128, 128))
    across = along.T
    same = across == along
    row_rank = jnp.sum(jnp.where(same & (iota((128, 128), 0) < iota((128, 128), 1)), 1.0, 0.0), axis=0, keepdims=True)
    col_rank = jnp.sum(jnp.where(same & (iota((128, 128), 1) < iota((128, 128), 0)), 1.0, 0.0), axis=1, keepdims=True)
    slots = 2.0 * along[:1] + row_rank
    slot_row[...] = jnp.broadcast_to(slots, (8, 128))
    slot_col[...] = 2.0 * across + col_rank
    ids = jnp.concatenate([support[...].astype(F32), jnp.zeros((126, 128), F32)], axis=0).T
    values = [points[axis] for axis in range(3)] + [normals[axis] for axis in range(3)]
    values = jnp.concatenate(values + [ids], axis=1)
    high = values.astype(BF16)
    rest = values - high.astype(F32)
    mid = rest.astype(BF16)
    low = (rest - mid.astype(F32)).astype(BF16)
    peers = iota((128, 128), 0).astype(F32)
    for rank in range(2):
        chosen = jnp.where(slots == 2.0 * peers + rank, 1.0, 0.0).astype(BF16)
        found = dot_nn(chosen, high) + dot_nn(chosen, mid) + dot_nn(chosen, low)
        for part in range(7):
            place = (3 * rank + part, 8 + 3 * rank + part - 3, 6 + rank)[
                0 if part < 3 else 1 if part < 6 else 2
            ]
            geo[pl.ds(place, 128, stride=16), :] = found[:, part * 128 : part * 128 + 128]
    for place in (14, 15):
        geo[pl.ds(place, 128, stride=16), :] = jnp.zeros((128, 128), F32)


def table_kernel(points, table):
    row = iota((8, 128), 0)
    zero = jnp.zeros((8, 128), F32)
    for block in range(8):
        tile = points[:, block, :] - 0.5
        size = jnp.broadcast_to(jnp.sum(tile * tile, axis=0, keepdims=True), (8, 128))
        size_high = size.astype(BF16).astype(F32)
        size_mid = (size - size_high).astype(BF16).astype(F32)
        size_low = size - size_high - size_mid
        sizes = jnp.where(
            row == 0, size_high, jnp.where(row == 1, size_mid, jnp.where(row == 2, size_low, 0.0))
        )
        for rank in range(2):
            pieces = [jnp.zeros((3, 128), F32)] * 2 + [jnp.zeros((2, 128), F32)]
            pieces[rank] = -2.0 * tile
            full = jnp.concatenate(pieces, axis=0) + jnp.where(row == 6 + rank, 1.0, 0.0)
            high = full.astype(BF16).astype(F32)
            mid = (full - high).astype(BF16).astype(F32)
            low = full - high - mid
            stack = jnp.concatenate(
                [high, mid, low, high, mid, high, sizes, zero] + [zero] * 8, axis=0
            )
            table[rank * 8 + block] = stack.T[:, :64].astype(BF16)


def spread_field(field, wide):
    for block in range(8):
        wide[block] = stacked_halves(field[pl.ds(block * 8, 8), :])


def moved_row(wide, tile, blocks, normal):
    left = jnp.concatenate([wide[block] for block in blocks], axis=1)
    moved = dot_nn(left, tile)
    moved = moved[:, :128] + moved[:, 128:]
    moved = moved[:3] + moved[8:11]
    return jnp.sum(moved * normal, axis=0, keepdims=True)


def tile_copy(source, target, sems, step):
    part = pl.ds(pl.multiple_of(step * 2 * PEERS, 2 * PEERS), 2 * PEERS)
    return pltpu.make_async_copy(source.at[part], target.at[part], sems.at[step])


def fetch_tiles(phi_hbm, phi, sems):
    def begin(step, carry):
        tile_copy(phi_hbm, phi, sems, step).start()
        return carry

    lax.fori_loop(0, STEPS, begin, 0)


def phi_kernel(support, geo, table, field, phi_hbm, motion, wide, phi, sems):
    spread_field(field, wide)
    row = iota((8, 128), 0)

    def body(step, carry):
        rows = []
        for peer in range(PEERS):
            start = pl.multiple_of((step * PEERS + peer) * 16, 16)
            tile = geo[pl.ds(start, 8), :] - 0.5
            normals = geo[pl.ds(start + 8, 8), :]
            square = tile * tile
            first = jnp.sum(jnp.where(row < 3, square, 0.0), axis=0, keepdims=True)
            second = jnp.sum(jnp.where((row >= 3) & (row < 6), square, 0.0), axis=0, keepdims=True)
            places = jnp.where(row < 6, tile, jnp.where(row == 6, first, second))
            high = places.astype(BF16).astype(F32)
            mid = (places - high).astype(BF16).astype(F32)
            low = places - high - mid
            ones = jnp.ones((8, 128), F32)
            right = jnp.concatenate(
                [high, high, high, mid, mid, low, ones, jnp.zeros((8, 128), F32)], axis=0
            ).astype(BF16)
            for rank in range(2):
                slot = (step * PEERS + peer) * 2 + rank
                blocks = [support[slot * 2 + k] for k in range(2)]
                left = jnp.concatenate([table[rank * 8 + block] for block in blocks], axis=0)
                squared = jnp.maximum(dot_nn(left, right), 1e-30)
                ratio = squared * lax.rsqrt(squared)
                reach = jnp.maximum(1.0 - ratio, 0.0)
                reach = reach * reach
                value = reach * reach * (4.0 * ratio + 1.0)
                tile = jnp.concatenate(halves(value), axis=1)
                phi[slot] = tile
                rows.append(moved_row(wide, tile, blocks, normals[3 * rank : 3 * rank + 3]))
        motion[pl.ds(pl.multiple_of(step * 2 * PEERS, 8), 8), :] = jnp.concatenate(rows, axis=0)
        tile_copy(phi, phi_hbm, sems, step).start()
        return carry

    lax.fori_loop(0, STEPS, body, 0)

    def finish(step, carry):
        tile_copy(phi, phi_hbm, sems, step).wait()
        return carry

    lax.fori_loop(0, STEPS, finish, 0)


def basis_kernel(first, support, geo, field, start, image, responses, phi_hbm, motion, wide, phi, sems):
    def copy(step):
        there = pl.ds(pl.multiple_of((first + step) * 2 * PEERS, 2 * PEERS), 2 * PEERS)
        here = pl.ds(pl.multiple_of(step * 2 * PEERS, 2 * PEERS), 2 * PEERS)
        return pltpu.make_async_copy(phi_hbm.at[there], phi.at[here], sems.at[step])

    def begin(step, carry):
        copy(step).start()
        return carry

    lax.fori_loop(0, STEPS // 2, begin, 0)
    for block in range(8):
        pieces = []
        for axis in range(3):
            line = pl.ds(block * 8 + axis, 1)
            rows = [field[line, :], start[line, :], image[line, :]]
            rows += [responses[h, line, :] for h in range(8)]
            pieces.append(jnp.concatenate(rows + [jnp.zeros((5, 128), F32)], axis=0))
        wide[block] = stacked_halves(jnp.concatenate(pieces, axis=0))

    def body(step, carry):
        copy(step).wait()
        for index in range(2 * PEERS):
            here = step * PEERS * 2 + index
            slot = first * PEERS * 2 + here
            rank = index % 2
            place = pl.multiple_of(((first + step) * PEERS + index // 2) * 16, 16)
            normals = geo[pl.ds(place + 8, 8), :]
            left = jnp.concatenate([wide[support[slot * 2 + k]] for k in range(2)], axis=1)
            moved = dot_nn(left, phi[here])
            moved = moved[:, :128] + moved[:, 128:]
            moved = moved[:48] + moved[48:]
            total = moved[:16] * normals[3 * rank : 3 * rank + 1]
            for axis in range(1, 3):
                line = 3 * rank + axis
                total = total + moved[16 * axis : 16 * axis + 16] * normals[line : line + 1]
            motion[here] = total
        return carry

    lax.fori_loop(0, STEPS // 2, body, 0)


def wall_kernel(received, slot_row, slot_col, bottom, base, fresh, sent):
    lanes = iota((128, 256), 1).astype(F32)
    column = jnp.concatenate([slot_col[...], slot_col[...]], axis=1)
    argument = exact_dot(jnp.where(column == lanes, 1.0, 0.0), received[...])
    wall = WALL_SPEED * jnp.tanh(WALL_GAIN * argument)
    lower = [bottom[part] for part in range(5)]
    ghost = [lower[0], lower[1], lower[2], 2.0 * lower[0] * wall - lower[3], lower[4]]
    inverse = 1.0 / lower[0]

    def terms(state):
        velocity = state[3] * inverse
        pressure = 0.4 * (
            state[4]
            - 0.5 * (state[1] * state[1] + state[2] * state[2] + state[3] * state[3]) * inverse
        )
        flux = [part * velocity for part in state]
        flux[3] = flux[3] + pressure
        flux[4] = flux[4] + pressure * velocity
        return flux, jnp.abs(velocity) + jnp.sqrt(1.4 * pressure * inverse)

    ghost_flux, ghost_speed = terms(ghost)
    lower_flux, lower_speed = terms(lower)
    speed = jnp.maximum(ghost_speed, lower_speed)
    new = []
    for part in range(5):
        face = 0.5 * (ghost_flux[part] + lower_flux[part])
        if part == 3:
            face = face - 0.5 * speed * (lower[3] - ghost[3])
        new.append(base[part] + STEP_RATIO * face)
        fresh[part] = new[part]
    pressure = 0.4 * (
        new[4] - 0.5 * (new[1] * new[1] + new[2] * new[2] + new[3] * new[3]) / new[0]
    )
    amount = -LOAD_SCALE * (pressure - PRESSURE_REF)
    chosen = jnp.where(slot_row[:1] == iota((256, 128), 0).astype(F32), 1.0, 0.0)
    sent[...] = exact_dot(chosen, amount)


def spread_back(values, couplings, pattern, total):
    total[...] = jnp.zeros((64, 128), F32)

    def body(block, carry):
        stack = stacked_halves(values[pl.ds(pl.multiple_of(block * 8, 8), 8), :])
        for k in range(4):
            upper, lower = halves(couplings[block, k])
            term = dot_nn(stack, upper) + dot_nn(stack, lower)
            place = pl.ds(pl.multiple_of(pattern[block * 4 + k] * 8, 8), 8)
            total[place, :] = total[place, :] + term[:8] + term[8:]
        return carry

    lax.fori_loop(0, 8, body, 0)


def gather_forward(values, couplings, pattern, total):
    def body(block, carry):
        term = jnp.zeros((16, 128), F32)
        for k in range(4):
            place = pl.ds(pl.multiple_of(pattern[block * 4 + k] * 8, 8), 8)
            stack = stacked_halves(values[place, :])
            upper, lower = halves(couplings[block, k])
            term = term + dot_nt(stack, upper) + dot_nt(stack, lower)
        total[pl.ds(pl.multiple_of(block * 8, 8), 8), :] = term[:8] + term[8:]
        return carry

    lax.fori_loop(0, 8, body, 0)


def back_kernel(pattern, values, couplings, total):
    spread_back(values, couplings, pattern, total)


def loads_kernel(
    support, pattern, amounts, geo, phi_hbm, base, couplings, start, back, l0, l1, l2, l3, phi, sems
):
    fetch_tiles(phi_hbm, phi, sems)
    for loads in (l0, l1, l2, l3):
        loads[...] = jnp.zeros((8, 8, 128), F32)
    row = iota((8, 128), 0)

    def body(step, carry):
        tile_copy(phi_hbm, phi, sems, step).wait()
        forces = amounts[pl.ds(pl.multiple_of(step * 2 * PEERS, 8), 8), :]
        for peer in range(PEERS):
            place = pl.multiple_of((step * PEERS + peer) * 16, 16)
            tile = geo[pl.ds(place + 8, 8), :]
            for rank in range(2):
                index = peer * 2 + rank
                slot = step * PEERS * 2 + index
                kept = (row >= 3 * rank) & (row < 3 * rank + 3)
                stack = stacked_halves(jnp.where(kept, tile * forces[index : index + 1], 0.0))
                stack = jnp.concatenate([stack, stack], axis=1)
                term = dot_nt(stack, phi[slot])
                term = term[:8] + term[8:]
                for k in range(2):
                    block = support[slot * 2 + k]
                    loads = ((l0, l1), (l2, l3))[rank][k]
                    loads[block] = loads[block] + term[:, k * 128 : k * 128 + 128]
        return carry

    lax.fori_loop(0, STEPS, body, 0)
    for block in range(8):
        tile = (l0[block] + l1[block]) + (l2[block] + l3[block])
        start[pl.ds(block * 8, 8), :] = base[pl.ds(block * 8, 8), :] + jnp.where(
            row < 3, tile + pltpu.roll(tile, 5, 0), 0.0
        )
    spread_back(start, couplings, pattern, back)


def apply_kernel(shift, pattern, values, before, behind, diagonal, couplings, image, work):
    gather_forward(before, couplings, pattern, work)
    image[...] = (diagonal[...] - shift) * values[...] - (1.0 / 1024.0) * (
        work[...] + behind[...]
    )


def row_sum(value):
    return jnp.sum(value, axis=0, keepdims=True)


def sums_kernel(
    pattern, start, image, before, diagonal, couplings, tested, extra, own, row, work, stack
):
    gather_forward(before, couplings, pattern, work)
    first, second = start[...], image[...]
    stack[...] = jnp.zeros((128, 128), F32)
    for h in range(8):
        stack[pl.ds(h, 1), :] = row_sum(tested[h] * first)
        stack[pl.ds(8 + h, 1), :] = row_sum(tested[h] * second)
    third = second * ((diagonal[...] - SHIFT) * second - (2.0 / 1024.0) * work[...])
    stack[pl.ds(16, 1), :] = row_sum(first * first)
    stack[pl.ds(17, 1), :] = row_sum(first * second)
    stack[pl.ds(18, 1), :] = row_sum(second * second)
    stack[pl.ds(19, 1), :] = row_sum(third)
    stack[pl.ds(20, 1), :] = row_sum(extra[...] * first)
    stack[pl.ds(21, 1), :] = row_sum(extra[...] * second)
    sums = jnp.sum(stack[...], axis=1, keepdims=True)
    row[...] = jnp.broadcast_to(sums, (128, 128)).T + own[...]


def solve_kernel(
    count, received, memory, field, start, image, last, responses, *more
):
    if count == 0:
        halves_of, (estimate, residual, kept, saved, motion) = more[:2], more[2:]
    else:
        estimate, residual = more
    totals = row_sum(received[...])

    def lane(index):
        return totals[:, index : index + 1]

    lanes, row = iota((8, 128), 1), iota((8, 128), 0)

    def column(values):
        return jnp.sum(
            jnp.where(lanes == row, jnp.broadcast_to(values, (8, 128)), 0.0), axis=1, keepdims=True
        )

    m0, m1, m2, m3 = lane(16), lane(17), lane(18), lane(19)
    alpha = m0 / (m1 + SHIFT * m0)
    gain = 1.0 - alpha * SHIFT
    norm = gain * gain * m0 - 2.0 * gain * alpha * m1 + alpha * alpha * m2
    mix = gain + norm / m0
    curve = (
        mix * mix * (m1 + SHIFT * m0)
        - 2.0 * mix * alpha * (m2 + SHIFT * m1)
        + alpha * alpha * (m3 + SHIFT * m2)
    )
    follow = norm / curve
    c0 = alpha + follow * mix
    c1 = -follow * alpha
    change = c0 * start[...] + c1 * image[...]
    response = field[...] + change
    size = c0 * c0 * m0 + 2.0 * c0 * c1 * m1 + c1 * c1 * m2
    projected = c0 * totals + c1 * pltpu.roll(totals, 120, 1)
    lane_row = iota((1, 128), 1)
    if count == 0:
        picked = jnp.where(
            (lanes >= 64 + 8 * row) & (lanes < 72 + 8 * row),
            jnp.broadcast_to(totals, (8, 128)),
            0.0,
        )
        fold = jnp.where(
            (iota((128, 128), 0) >= 64) & (iota((128, 128), 0) % 8 == iota((128, 128), 1)), 1.0, 0.0
        )
        gram = exact_dot(picked, fold)
    else:
        overlap = c0 * lane(20) + c1 * lane(21)
        newest = size - overlap
        edge = projected - memory[8:9, :]
        edge = jnp.where(lane_row == 0, newest - overlap + memory[9:10, :1], edge)
        projected = jnp.where(lane_row == 0, newest, projected)
        gram = jnp.where(
            row == 0, jnp.broadcast_to(edge, (8, 128)), jnp.where(lanes == 0, column(edge), memory[:8, :])
        )
    system = jnp.where(lanes < 8, gram, jnp.where(lanes == 8, column(projected), 0.0))
    for j in range(8):
        pivot = system[j : j + 1] / system[j : j + 1, j : j + 1]
        system = jnp.where(row == j, pivot, system - system[:, j : j + 1] * pivot)
    result = response
    for h in range(8):
        weight = system[h : h + 1, 8:9]
        used = responses[h] if count == 0 or h > 0 else response - last[...]
        result = result - weight * used
    if count == 0:
        one = jnp.ones((1, 1), F32)
        mixture = jnp.concatenate(
            [one, c0, c1, -system[:, 8:9], jnp.zeros((5, 1), F32)], axis=0
        )
        mixture = jnp.broadcast_to(mixture, (16, 128))
        for half in range(2):
            for chunk in range(16):
                tiles = halves_of[half][chunk * 8 : chunk * 8 + 8]
                place = half * 128 + chunk * 8
                motion[place : place + 8, :] = jnp.sum(tiles * mixture[None], axis=1)
        estimate[...] = result
        residual[...] = change
        kept[...] = response
        saved[:8, :] = gram
        saved[8:16, :] = jnp.where(
            row == 0, jnp.broadcast_to(projected, (8, 128)), jnp.where(row == 1, size, 0.0)
        )
    else:
        for block in range(8):
            for axis in range(3):
                line = block * 8 + axis
                estimate[axis, block : block + 1, :] = result[line : line + 1]
                residual[axis, block : block + 1, :] = change[line : line + 1]


def shape(*dims, dtype=F32):
    return jax.ShapeDtypeStruct(dims, dtype)


def call(kernel, outs, scratch=(), scalars=0, cost=None, room=14, **kw):
    specs = [pl.BlockSpec(memory_space=SMEM)] * scalars

    def run(*args):
        return pl.pallas_call(
            kernel,
            out_shape=outs,
            in_specs=specs + [pl.BlockSpec()] * (len(args) - scalars),
            out_specs=jax.tree.map(lambda _: pl.BlockSpec(), outs),
            scratch_shapes=list(scratch),
            compiler_params=pltpu.CompilerParams(vmem_limit_bytes=room << 20),
            cost_estimate=cost,
            **kw,
        )(*args)

    return run


def exchange(values):
    return lax.all_to_all(values, AXES, split_axis=0, concat_axis=0, tiled=True)


def forward(values):
    return lax.ppermute(values, AXES, [(i, (i + 1) % DEVICES) for i in range(DEVICES)])


def backward(values):
    return lax.ppermute(values, AXES, [((i + 1) % DEVICES, i) for i in range(DEVICES)])


def shift(values, axis, step):
    count = lax.axis_size(axis)
    return lax.ppermute(values, axis, [(i, (i + step) % count) for i in range(count)])


STEPS = DEVICES // PEERS
WIDE = pltpu.VMEM((8, 16, 128), BF16)
PHI_COST = pl.CostEstimate(flops=2_000_000_000, bytes_accessed=40_000_000, transcendentals=0)
RESIDENT = pl.BlockSpec(memory_space=pl.ANY)
HELD = [pltpu.VMEM((256, 256, 256), BF16), pltpu.SemaphoreType.DMA((DEVICES // PEERS,))]


def whole(kernel, scalars, in_specs, out_specs, outs, scratch, args):
    return pl.pallas_call(
        kernel,
        out_shape=outs,
        in_specs=[pl.BlockSpec(memory_space=SMEM)] * scalars + in_specs,
        out_specs=out_specs,
        scratch_shapes=scratch,
        compiler_params=pltpu.CompilerParams(vmem_limit_bytes=56 << 20),
        cost_estimate=PHI_COST,
    )(*args)


def build_phi(support, geo, table, field):
    return whole(
        phi_kernel,
        1,
        [pl.BlockSpec()] * 3,
        [RESIDENT, pl.BlockSpec()],
        [shape(256, 256, 256, dtype=BF16), shape(256, 128)],
        [WIDE] + HELD,
        (support, geo, table, field),
    )


def basis_motion(half, support, geo, field, start, image, responses, phi):
    return whole(
        functools.partial(basis_kernel, half * STEPS // 2),
        1,
        [pl.BlockSpec()] * 5 + [RESIDENT],
        pl.BlockSpec(),
        shape(128, 16, 128),
        [
            pltpu.VMEM((8, 96, 128), BF16),
            pltpu.VMEM((128, 256, 256), BF16),
            pltpu.SemaphoreType.DMA((STEPS // 2,)),
        ],
        (support, geo, field, start, image, responses, phi),
    )


def find_loads(support, pattern, amounts, geo, phi, base, couplings):
    return whole(
        loads_kernel,
        2,
        [pl.BlockSpec()] * 2 + [RESIDENT] + [pl.BlockSpec()] * 2,
        [pl.BlockSpec(), pl.BlockSpec()],
        [shape(64, 128), shape(64, 128)],
        [pltpu.VMEM((8, 8, 128), F32)] * 4 + HELD,
        (support, pattern, amounts, geo, phi, base, couplings),
    )


def padded(values):
    wide = [(0, 0)] * (values.ndim - 2) + [(0, 5), (0, 0)]
    values = jnp.pad(values, wide)
    return values.reshape(values.shape[:-3] + (64, 128))


def on_device(
    fluid_state,
    surface_points,
    surface_normals,
    owner_ids,
    support_ids,
    struct_points,
    couplings,
    coupling_pattern,
    stiff_diagonal,
    struct_load,
    predicted,
    hist_residual,
    hist_response,
):
    pattern = coupling_pattern.reshape(32)
    geo, slot_row, slot_col = call(
        pack_kernel, [shape(2048, 128), shape(8, 128), shape(128, 128)], room=56
    )(
        owner_ids.T,
        jnp.transpose(surface_points, (1, 0, 2)),
        jnp.transpose(surface_normals, (1, 0, 2)),
        support_ids.T,
    )
    geo = exchange(geo)
    support = geo.reshape(128, 16, 128)[:, 6:8, :2].astype(jnp.int32).reshape(512)
    low_x, high_x, low_y, high_y = call(edges_kernel, [shape(40, 128)] * 4)(fluid_state)
    sides = [
        shift(low_x, "fx", -1),
        shift(high_x, "fx", 1),
        shift(low_y, "fy", -1),
        shift(high_y, "fy", 1),
    ]
    diagonal = padded(jnp.broadcast_to(stiff_diagonal[:, None, :], (8, 3, 128)))
    load = padded(struct_load)
    field = padded(predicted)
    tested = padded(hist_residual)
    responses = padded(hist_response)
    own = jnp.pad(
        jnp.einsum("hbdp,gbdp->hg", hist_residual, hist_residual, precision=TOP_PRECISION).reshape(
            1, 64
        ),
        ((0, 0), (64, 0)),
    )
    table = call(table_kernel, shape(16, 128, 64, dtype=BF16))(
        jnp.transpose(struct_points, (1, 0, 2))
    )

    def back_of(values):
        return call(back_kernel, shape(64, 128), scalars=1)(pattern, values, couplings)

    def applied(values, back, shift, gate=None):
        before = forward(values)
        if gate is not None:
            back, before = lax.optimization_barrier((back, before))
            values = lax.optimization_barrier((values, gate))[0]
        behind = backward(back)
        return call(
            functools.partial(apply_kernel, shift),
            shape(64, 128),
            [pltpu.VMEM((64, 128), F32)],
            scalars=1,
        )(pattern, values, before, behind, diagonal, couplings)

    phi, motion = build_phi(support, geo, table, field)
    halos, motion = lax.optimization_barrier(
        ((sides[1], sides[0], sides[3], sides[2]), motion)
    )

    def fluid(levels, gate=None):
        ends = halos
        if gate is not None:
            ends, _ = lax.optimization_barrier((halos, gate))
        return call(
            functools.partial(fluid_kernel, levels),
            shape(5, len(levels), 128, 128),
            [pltpu.VMEM((4, 5, 128, 128), F32)],
            cost=pl.CostEstimate(
                flops=len(levels) * 40_000_000, bytes_accessed=len(levels) * 700_000, transcendentals=0
            ),
        )(fluid_state, *ends)

    bottom = fluid_state[:, 0]
    base_bottom = fluid((0,)).reshape(5, 128, 128)
    fluid_parts = []
    extra = field
    memory = diagonal
    last = field
    for count in range(2):
        received = exchange(motion)
        fresh, sent = call(wall_kernel, [shape(5, 128, 128), shape(256, 128)])(
            received, slot_row, slot_col, bottom, base_bottom
        )
        amounts = exchange(sent)
        ready = lax.optimization_barrier((field, motion))[0]
        stiff = applied(ready, back_of(ready), 0.0, sent)
        base = load - stiff
        if count == 0:
            fluid_parts.append(fluid((1, 2, 3), sent))
            amounts, fluid_parts[0] = lax.optimization_barrier((amounts, fluid_parts[0]))
        start, back = find_loads(support, pattern, amounts, geo, phi, base, couplings)
        image = applied(start, back, SHIFT)
        ahead = forward(image)
        if count == 0:
            first_half = basis_motion(0, support, geo, field, start, image, responses, phi)
            ahead, first_half = lax.optimization_barrier((ahead, first_half))
        else:
            fluid_parts.append(fluid((4, 5, 6, 7), image))
            ahead, fluid_parts[-1] = lax.optimization_barrier((ahead, fluid_parts[-1]))
        row = call(
            sums_kernel,
            shape(128, 128),
            [pltpu.VMEM((64, 128), F32), pltpu.VMEM((128, 128), F32)],
            scalars=1,
        )(
            pattern,
            start,
            image,
            ahead,
            diagonal,
            couplings,
            tested,
            extra,
            own if count == 0 else jnp.zeros_like(own),
        )
        totals = exchange(row)
        if count == 0:
            gated = lax.optimization_barrier((start, image, row))
            final_half = basis_motion(
                1, support, geo, field, gated[0], gated[1], responses, phi
            )
            totals, final_half = lax.optimization_barrier((totals, final_half))
        solve = functools.partial(solve_kernel, count)
        if count == 0:
            outs = [shape(64, 128)] * 3 + [shape(16, 128), shape(256, 128)]
            field, extra, last, memory, motion = call(solve, outs, room=56)(
                totals,
                jnp.zeros((16, 128), F32),
                field,
                start,
                image,
                last,
                responses,
                first_half,
                final_half,
            )
        else:
            outs = [shape(3, 8, 128), shape(3, 8, 128)]
            estimate, residual = call(solve, outs)(
                totals, memory, field, start, image, last, responses
            )
    new_state = jnp.concatenate([fresh[:, None]] + fluid_parts, axis=1)
    return (
        new_state,
        jnp.transpose(estimate, (1, 0, 2)),
        jnp.transpose(residual, (1, 0, 2)),
    )


def solution(mesh):
    placed = (
        P(None, None, "fx", "fy"),
        P(("fx", "fy"), None, None),
        P(("fx", "fy"), None, None),
        P(("fx", "fy"), None),
        P(("fx", "fy"), None),
        P(("fx", "fy"), None, None),
        P(("fx", "fy"), None, None, None),
        P(("fx", "fy"), None),
        P(("fx", "fy"), None),
        P(("fx", "fy"), None, None),
        P(("fx", "fy"), None, None),
        P(None, ("fx", "fy"), None, None),
        P(None, ("fx", "fy"), None, None),
    )
    return jax.shard_map(
        on_device,
        mesh=mesh,
        in_specs=placed,
        out_specs=(
            P(None, None, "fx", "fy"),
            P(("fx", "fy"), None, None),
            P(("fx", "fy"), None, None),
        ),
        check_vma=False,
    )
```
